32 devices in a mesh: dp: 4 (over y, core), mp: 8 (over z, x).
Axes of the slice: x: 2, y: 2, z: 4, core: 2. Of those that a mesh axis runs over, the one named last changes fastest.
Arguments:
- features: bfloat16 [8, 24, 24, 1024], P('dp'), may hold values from -6 to 6
- w_in: bfloat16 [2, 1024, 1024], P(None, 'mp'), may hold values from -0.1875 to 0.1875
- ln_gain: float32 [2, 1024], P(None, 'mp'), may hold values from 0.5 to 1.5
- ln_bias: float32 [2, 1024], P(None, 'mp'), may hold values from -3 to 3
- w_conv: bfloat16 [2, 1024, 9, 1024], P(None, 'mp')
- se_down: bfloat16 [2, 1024, 256], P(None, 'mp'), may hold values from -0.375 to 0.375
- se_down_bias: float32 [2, 256], replicated, may hold values from -3 to 3
- se_up: bfloat16 [2, 256, 1024], P(None, None, 'mp'), may hold values from -0.375 to 0.375
- se_up_bias: float32 [2, 1024], P(None, 'mp'), may hold values from -3 to 3
- w_out: bfloat16 [2, 1024, 1024], P(None, 'mp'), may hold values from -0.375 to 0.375
- w_read1: bfloat16 [1024, 4096], P(None, 'mp'), may hold values from -0.1875 to 0.1875
- b_read1: float32 [4096], P('mp'), may hold values from -3 to 3
- w_read2: bfloat16 [4096, 4096], P('mp'), may hold values from -0.09375 to 0.09375
- b_read2: float32 [4096], P('mp'), may hold values from -3 to 3
- out_grad: bfloat16 [8, 12, 12, 4096], P('dp', None, None, 'mp'), may hold values from -6 to 6
- box_counts: int32 [8], P('dp'), may hold values from 1 to 4
Outputs:
- readout: bfloat16 [8, 12, 12, 4096], P('dp', None, None, 'mp')
- grad_features: float32 [8, 24, 24, 1024], P('dp', None, None, 'mp')
- grad_w_in: float32 [2, 1024, 1024], P(None, 'mp', 'dp')
- grad_ln_gain: float32 [2, 1024], P(None, 'mp')
- grad_ln_bias: float32 [2, 1024], P(None, 'mp')
- grad_w_conv: float32 [2, 1024, 9, 1024], P(None, 'mp', None, 'dp')
- grad_se_down: float32 [2, 1024, 256], P(None, 'mp', 'dp')
- grad_se_down_bias: float32 [2, 256], replicated
- grad_se_up: float32 [2, 256, 1024], P(None, 'dp', 'mp')
- grad_se_up_bias: float32 [2, 1024], P(None, 'mp')
- grad_w_out: float32 [2, 1024, 1024], P(None, 'mp', 'dp')
- grad_w_read1: float32 [1024, 4096], P('dp', 'mp')
- grad_b_read1: float32 [4096], P('mp')
- grad_w_read2: float32 [4096, 4096], P('mp', 'dp')
- grad_b_read2: float32 [4096], P('mp')
The draws below stay inside these ranges and needn't reach their ends.
All inputs are finite; a program needn't handle non-finite values.
Results may differ from the reference program's by a relative error of at most 0.017.
Values may be sent and summed in bfloat16 or wider, within the bound.
A program may use at most 128 MiB of HBM per device.

```python
import math
import jax
import jax.numpy as jnp
from jax import lax

SIDE = 24
WIDTH = 1024
SQUEEZE = 256
READ_HIDDEN = 4096
OUTW = 4096
BLOCKS = 2
POOLED = 12
IMAGES = 8


def draw_w_conv(key, part):
    spread = (9.0 * WIDTH) ** (-0.5)
    noise_key = jax.random.fold_in(key, 7101)
    common_key = jax.random.fold_in(key, 7102)
    noise = jax.random.truncated_normal(noise_key, -4.0, 4.0, (BLOCKS, WIDTH, 9, WIDTH), jnp.float32) * spread
    common = jax.random.truncated_normal(common_key, -4.0, 4.0, (BLOCKS, WIDTH, 9, 1), jnp.float32) * (0.5 * spread)
    return (noise + common).astype(jnp.bfloat16)


def place_ends(values, key, low, top_value):
    place = [jax.random.randint(jax.random.fold_in(key, axis), (), 0, length) for axis, length in enumerate(values.shape)]
    widest = values.shape.index(max(values.shape))
    neighbour = place[:widest] + [(place[widest] + 1) % values.shape[widest]] + place[widest + 1:]
    return values.at[tuple(place)].set(low).at[tuple(neighbour)].set(top_value)


def block_scale(own_key, extent, split, low, largest):
    level, own = 1.0, jax.random.fold_in(own_key, 6)
    for position, blocks in split:
        heights = jnp.exp(jax.random.uniform(jax.random.fold_in(own, position), (blocks,), jnp.float32, low / len(split), largest / len(split)))
        level = level * jnp.repeat(heights, extent[position] // blocks).reshape([-1 if axis == position else 1 for axis in range(len(extent))])
    return level


def bell_draw(own_key, extent, deviation, bound, cuts=(), dtype=jnp.bfloat16):
    values = deviation * jax.random.normal(own_key, extent, jnp.float32)
    if cuts:
        values = values * block_scale(own_key, extent, cuts, -0.22, 0.18)
    return jnp.clip(values, -bound, bound).astype(dtype)


def setup_inputs(seed: int = 0) -> dict:
    keys = jax.random.split(jax.random.key(seed), 17)
    features = bell_draw(keys[0], (IMAGES, SIDE, SIDE, WIDTH), 1.0, 6.0, ((0, 4),))
    w_in = bell_draw(keys[1], (BLOCKS, WIDTH, WIDTH), WIDTH ** -0.5, 0.1875, ((1, 8),))
    ln_gain = jnp.clip(1.0 + 0.1 * jax.random.normal(keys[2], (BLOCKS, WIDTH), jnp.float32), 0.5, 1.5)
    ln_bias = bell_draw(keys[3], (BLOCKS, WIDTH), 0.5, 3.0, ((1, 8),), jnp.float32)
    w_conv = draw_w_conv(jax.random.fold_in(keys[16], 71), 0)
    se_down = bell_draw(keys[5], (BLOCKS, WIDTH, SQUEEZE), (WIDTH // 4) ** -0.5, 0.375, ((1, 8),))
    se_down_bias = bell_draw(keys[6], (BLOCKS, SQUEEZE), 0.5, 3.0, (), jnp.float32)
    se_up = bell_draw(keys[7], (BLOCKS, SQUEEZE, WIDTH), SQUEEZE ** -0.5, 0.375, ((2, 8),))
    se_up_bias = bell_draw(keys[8], (BLOCKS, WIDTH), 0.5, 3.0, ((1, 8),), jnp.float32)
    w_out = bell_draw(keys[9], (BLOCKS, WIDTH, WIDTH), (WIDTH // 4) ** -0.5, 0.375, ((1, 8),))
    w_read1 = bell_draw(keys[10], (WIDTH, READ_HIDDEN), WIDTH ** -0.5, 0.1875, ((1, 8),))
    b_read1 = bell_draw(keys[11], (READ_HIDDEN,), 0.5, 3.0, ((0, 8),), jnp.float32)
    w_read2 = bell_draw(keys[12], (READ_HIDDEN, OUTW), READ_HIDDEN ** -0.5, 0.09375, ((0, 8),))
    b_read2 = bell_draw(keys[13], (OUTW,), 0.5, 3.0, ((0, 8),), jnp.float32)
    out_grad = bell_draw(keys[14], (IMAGES, POOLED, POOLED, OUTW), 1.0, 6.0, ((0, 4), (3, 8)))
    box_counts = place_ends(jax.random.randint(keys[15], (IMAGES,), 1, 5), jax.random.fold_in(keys[15], 1), 1, 4).astype(jnp.int32)
    return dict(features=features, w_in=w_in, ln_gain=ln_gain, ln_bias=ln_bias, w_conv=w_conv, se_down=se_down, se_down_bias=se_down_bias, se_up=se_up, se_up_bias=se_up_bias, w_out=w_out, w_read1=w_read1, b_read1=b_read1, w_read2=w_read2, b_read2=b_read2, out_grad=out_grad, box_counts=box_counts)


@jax.custom_vjp
def low(v):
    return lax.optimization_barrier(v.astype(jnp.bfloat16)).astype(jnp.float32)

@jax.custom_vjp
def low_back(v):
    return v

def low_keep(v):
    return (low(v), None)

def low_pass(kept, grad):
    return (grad,)

def back_keep(v):
    return (v, None)

def back_low(kept, grad):
    return (low(grad),)
low.defvjp(low_keep, low_pass)
low_back.defvjp(back_keep, back_low)
epsilon = 1e-06
highest = lax.Precision.HIGHEST

def product(left, weight):
    return jnp.einsum('bijc,cd->bijd', left, weight, precision=highest)

def product_t(left, weight):
    return jnp.einsum('bijc,dc->bijd', left, weight, precision=highest)

def conv_three(value, weight):
    grid_side = value.shape[1]
    padded = jnp.pad(value, ((0, 0), (1, 1), (1, 1), (0, 0)))
    result = jnp.zeros(value.shape[:3] + (weight.shape[0],), jnp.float32)
    for offset in range(9):
        down_shift = offset // 3
        right_shift = offset % 3
        result = result + product_t(padded[:, down_shift:down_shift + grid_side, right_shift:right_shift + grid_side, :], weight[:, offset, :])
    return result

def res_block(value, w_in, gain, shift, w_conv, se_down, se_down_bias, se_up, se_up_bias, w_out):
    reduced = low_back(product_t(low(value), w_in))
    row_mean = lax.optimization_barrier(jnp.mean(reduced, axis=3, keepdims=True))
    centered = reduced - row_mean
    row_var = lax.optimization_barrier(jnp.mean(centered * centered, axis=3, keepdims=True))
    normed = centered * lax.rsqrt(row_var + epsilon) * gain + shift
    conv_out = low_back(conv_three(low(normed), w_conv))
    activated = jax.nn.silu(conv_out)
    pooled = lax.optimization_barrier(jnp.mean(activated, axis=(1, 2)))
    squeeze = jax.nn.silu(jnp.dot(pooled, se_down, precision=highest) + se_down_bias)
    excite = jax.nn.sigmoid(jnp.dot(squeeze, se_up, precision=highest) + se_up_bias)
    scaled = activated * excite[:, None, None, :]
    return value + low_back(product_t(low(scaled), w_out))

def avg_pool(value):
    shape = value.shape
    return lax.optimization_barrier(jnp.mean(value.reshape(shape[0], shape[1] // 2, 2, shape[2] // 2, 2, shape[3]), axis=(2, 4)))

def forward(features, w_in, ln_gain, ln_bias, w_conv, se_down, se_down_bias, se_up, se_up_bias, w_out, w_read1, b_read1, w_read2, b_read2):

    def layer_weights(index):
        return (w_in[index], ln_gain[index], ln_bias[index], w_conv[index], se_down[index], se_down_bias[index], se_up[index], se_up_bias[index], w_out[index])

    def one_group(images):
        value = res_block(images, *layer_weights(0))
        value = res_block(avg_pool(value), *layer_weights(1))
        hidden = low_back(product(low(value), w_read1) + b_read1)
        active = jax.nn.gelu(hidden, approximate=False)
        return low_back(product(low(active), w_read2) + b_read2)
    count = features.shape[0]
    per_group = math.gcd(count, 4)
    grouped = features.reshape((count // per_group, per_group) + features.shape[1:])
    result = lax.map(jax.checkpoint(one_group), grouped)
    return result.reshape((count,) + result.shape[2:])

def reference(features, w_in, ln_gain, ln_bias, w_conv, se_down, se_down_bias, se_up, se_up_bias, w_out, w_read1, b_read1, w_read2, b_read2, out_grad, box_counts):
    primals = [array.astype(jnp.float32) for array in (features, w_in, ln_gain, ln_bias, w_conv, se_down, se_down_bias, se_up, se_up_bias, w_out, w_read1, b_read1, w_read2, b_read2)]
    result, pullback = jax.vjp(forward, *primals)
    cotangent = out_grad.astype(jnp.float32) * box_counts.astype(jnp.float32)[:, None, None, None]
    gradients = pullback(cotangent)
    return (result.astype(jnp.bfloat16), gradients[0], gradients[1], gradients[2], gradients[3], gradients[4], gradients[5], gradients[6], gradients[7], gradients[8], gradients[9], gradients[10], gradients[11], gradients[12], gradients[13])
```

```python
from functools import partial

import jax
import jax.numpy as jnp
from jax import lax
from jax.experimental import pallas as pl
from jax.experimental.pallas import tpu as pltpu
from jax.sharding import PartitionSpec as P

epsilon = 1e-06
highest = lax.Precision.HIGHEST
f32 = jnp.float32
bf16 = jnp.bfloat16
MESH = pl.DeviceIdType.MESH
VMEM_LIMIT = 56 << 20


def vmem_specs(count):
    return [pl.BlockSpec(memory_space=pltpu.VMEM)] * count


def barrier(peers):
    sem = pltpu.get_barrier_semaphore()
    for peer in peers:
        pl.semaphore_signal(sem, inc=1, device_id=peer, device_id_type=MESH)
    pl.semaphore_wait(sem, len(peers))


def sent(src, dst, send_sem, recv_sem, peer):
    return pltpu.make_async_remote_copy(
        src_ref=src,
        dst_ref=dst,
        send_sem=send_sem,
        recv_sem=recv_sem,
        device_id=peer,
        device_id_type=MESH,
    )


def exchange_kernel(size, kinds, *refs):
    count = len(kinds)
    sources, results = refs[:count], refs[count : 2 * count]
    slots = list(refs[2 * count : -2])
    send_sem, recv_sem = refs[-2:]
    landing = [slots.pop(0) if kind in ("rs", "psum") else result for kind, result in zip(kinds, results)]
    dp, mp = lax.axis_index("dp"), lax.axis_index("mp")
    peers = [(dp, lax.rem(mp + step, size)) for step in range(1, size)]
    barrier(peers)
    copies = []
    for index, kind in enumerate(kinds):
        for step, peer in enumerate(peers):
            src = sources[index].at[peer[1]] if kind in ("rs", "a2a") else sources[index]
            copy = sent(
                src, landing[index].at[mp], send_sem.at[index, step], recv_sem.at[index, step], peer
            )
            copy.start()
            copies.append(copy)
    for index, kind in enumerate(kinds):
        if kind in ("rs", "a2a"):
            landing[index][mp] = sources[index][mp]
        else:
            landing[index][mp] = sources[index][...]
    for copy in copies:
        copy.wait()
    for index, kind in enumerate(kinds):
        if kind in ("rs", "psum"):
            total = landing[index][0].astype(f32)
            for step in range(1, size):
                total = total + landing[index][step].astype(f32)
            results[index][...] = total


def exchange(name, collective, size, *pairs):
    kinds = tuple(kind for kind, value in pairs)
    values = [value for kind, value in pairs]
    shapes, scratch = [], []
    for kind, value in pairs:
        block = value.shape[1:] if kind in ("rs", "a2a") else value.shape
        if kind in ("rs", "psum"):
            shapes.append(jax.ShapeDtypeStruct(block, f32))
            scratch.append(pltpu.VMEM((size,) + block, value.dtype))
        else:
            shapes.append(jax.ShapeDtypeStruct((size,) + block, value.dtype))
    sems = pltpu.SemaphoreType.DMA((len(pairs), size - 1))
    return pl.pallas_call(
        partial(exchange_kernel, size, kinds),
        name=name,
        out_shape=shapes,
        in_specs=vmem_specs(len(values)),
        out_specs=vmem_specs(len(values)),
        scratch_shapes=scratch + [sems, sems],
        compiler_params=pltpu.CompilerParams(
            collective_id=collective, has_side_effects=True, vmem_limit_bytes=VMEM_LIMIT
        ),
    )(*values)


def weights_kernel(size, w_ref, gb_ref, out_ref, gb_out, ss, rs, cs, cr, gs, gr):
    dp, mp = lax.axis_index("dp"), lax.axis_index("mp")
    core = lax.rem(dp, 2)
    sibling = (dp + 1 - 2 * core, mp)
    peers = [(dp, lax.rem(mp + step, size)) for step in range(1, size)]
    barrier(peers + [sibling])
    count, rows = w_ref.shape[0], w_ref.shape[1]
    half = rows // 2
    mine = pl.ds(pl.multiple_of(core * half, half), half)

    def part(owner):
        return pl.ds(pl.multiple_of(owner * rows + core * half, half), half)

    copies = []
    for step, peer in enumerate(peers):
        copy = sent(gb_ref, gb_out.at[mp], gs.at[step], gr.at[step], peer)
        copy.start()
        copies.append(copy)
    outgoing = {}
    for which in range(count):
        for step, peer in enumerate(peers):
            copy = sent(
                w_ref.at[which, mine],
                out_ref.at[which, part(mp)],
                ss.at[which, step],
                rs.at[which, step],
                peer,
            )
            copy.start()
            outgoing[which, step] = copy
    gb_out[mp] = gb_ref[...]
    for which in range(count):
        out_ref[which, pl.ds(pl.multiple_of(mp * rows, rows), rows), :] = w_ref[which]
    for which in range(count):
        for step in range(size - 1):
            owner = lax.rem(mp + size - 1 - step, size)
            outgoing[which, step].wait_recv()
            copy = sent(
                out_ref.at[which, part(owner)],
                out_ref.at[which, part(owner)],
                cs.at[which, step],
                cr.at[which, step],
                sibling,
            )
            copy.start()
            copies.append(copy)
    for copy in outgoing.values():
        copy.wait_send()
    for copy in copies:
        copy.wait()


def gather_weights(size, weights, vectors):
    count, rows, width = weights.shape
    sem = pltpu.SemaphoreType.DMA((count, size - 1))
    vector_sem = pltpu.SemaphoreType.DMA((size - 1,))
    return pl.pallas_call(
        partial(weights_kernel, size),
        name="gather_weights",
        out_shape=[
            jax.ShapeDtypeStruct((count, rows * size, width), weights.dtype),
            jax.ShapeDtypeStruct((size,) + vectors.shape, vectors.dtype),
        ],
        in_specs=vmem_specs(2),
        out_specs=vmem_specs(2),
        scratch_shapes=[sem, sem, sem, sem, vector_sem, vector_sem],
        compiler_params=pltpu.CompilerParams(
            collective_id=1, has_side_effects=True, vmem_limit_bytes=VMEM_LIMIT
        ),
    )(weights, vectors)


def dp_kernel(size, *refs):
    count = (len(refs) - 4) // 4
    sources = refs[:count]
    results = refs[count : 2 * count]
    first = refs[2 * count : 3 * count]
    second = refs[3 * count : 4 * count]
    cs, cr, ys, yr = refs[4 * count :]
    dp, mp = lax.axis_index("dp"), lax.axis_index("mp")
    core = lax.rem(dp, 2)
    y = lax.div(dp, 2)
    chips = size // 2
    sibling = (dp + 1 - 2 * core, mp)
    others = [(2 * lax.rem(y + step, chips) + core, mp) for step in range(1, chips)]
    barrier([sibling] + others)
    copies = []
    for index in range(count):
        for chip in range(chips):
            copy = sent(
                sources[index].at[2 * chip + 1 - core],
                first[index].at[chip],
                cs.at[index, chip],
                cr.at[index, chip],
                sibling,
            )
            copy.start()
            copies.append(copy)
    late = []
    for index in range(count):
        for chip in range(chips):
            copies[index * chips + chip].wait_recv()
            first[index][chip] = (
                first[index][chip].astype(f32) + sources[index][2 * chip + core].astype(f32)
            ).astype(first[index].dtype)
        for step, peer in enumerate(others):
            copy = sent(
                first[index].at[lax.rem(y + step + 1, chips)],
                second[index].at[step],
                ys.at[index, step],
                yr.at[index, step],
                peer,
            )
            copy.start()
            late.append((index, copy))
    for index in range(count):
        total = first[index][y].astype(f32)
        for step in range(chips - 1):
            late[index * (chips - 1) + step][1].wait_recv()
            total = total + second[index][step].astype(f32)
        results[index][...] = total
    for copy in copies:
        copy.wait_send()
    for index, copy in late:
        copy.wait_send()


def dp_scatter(size, values):
    count, chips = len(values), size // 2
    first = [pltpu.VMEM((chips,) + value.shape[1:], value.dtype) for value in values]
    second = [pltpu.VMEM((max(chips - 1, 1),) + value.shape[1:], value.dtype) for value in values]
    core_sem = pltpu.SemaphoreType.DMA((count, chips))
    y_sem = pltpu.SemaphoreType.DMA((count, max(chips - 1, 1)))
    return pl.pallas_call(
        partial(dp_kernel, size),
        name="dp_scatter",
        out_shape=[jax.ShapeDtypeStruct(value.shape[1:], f32) for value in values],
        in_specs=vmem_specs(count),
        out_specs=vmem_specs(count),
        scratch_shapes=first + second + [core_sem, core_sem, y_sem, y_sem],
        compiler_params=pltpu.CompilerParams(
            collective_id=2, has_side_effects=True, vmem_limit_bytes=VMEM_LIMIT
        ),
    )(*values)


def nt(left, right):
    return lax.dot_general(left, right, (((1,), (1,)), ((), ())), preferred_element_type=f32)


def nn(left, right):
    return lax.dot_general(left, right, (((1,), (0,)), ((), ())), preferred_element_type=f32)


def tn(left, right):
    return lax.dot_general(left, right, (((0,), (0,)), ((), ())), preferred_element_type=f32)


def exact(left, right):
    return jnp.dot(left, right, precision=highest)


def blocks_to_wide(value):
    return jnp.swapaxes(value, 0, 1).reshape(value.shape[1], -1)


def wide_to_blocks(value, count):
    return jnp.swapaxes(value.reshape(value.shape[0], count, -1), 0, 1)


def normalize(h):
    mean = jnp.mean(h, axis=1, keepdims=True)
    centered = h - mean
    inv_std = lax.rsqrt(jnp.mean(centered * centered, axis=1, keepdims=True) + epsilon)
    return centered * inv_std, inv_std


def conv_forward(norm, w_conv, images, side):
    width = norm.shape[1]
    out = lax.conv_general_dilated(
        norm.reshape(images, side, side, width),
        w_conv.reshape(w_conv.shape[0], 3, 3, width),
        (1, 1),
        ((1, 1), (1, 1)),
        dimension_numbers=("NHWC", "OHWI", "NHWC"),
        preferred_element_type=f32,
    )
    return out.reshape(images, side * side, -1)


def shifted(grad_conv, images, side):
    width = grad_conv.shape[1]
    padded = jnp.pad(grad_conv.reshape(images, side, side, width), ((0, 0), (1, 1), (1, 1), (0, 0)))
    parts = [
        padded[:, 2 - tap // 3 : 2 - tap // 3 + side, 2 - tap % 3 : 2 - tap % 3 + side, :]
        for tap in range(9)
    ]
    return jnp.stack(parts, axis=3).reshape(images * side * side, 9 * width)


def pool(value, images, side):
    half = side // 2
    shape = (images, half, 2, half, 2, value.shape[-1])
    return jnp.mean(value.astype(f32).reshape(shape), axis=(2, 4)).reshape(images * half * half, -1)


def spread(value, images, half):
    grid = value.reshape(images, half, 1, half, 1, value.shape[-1])
    full = jnp.broadcast_to(grid, (images, half, 2, half, 2, value.shape[-1]))
    return full.reshape(images * 4 * half * half, -1)


def gelu_parts(value):
    cdf = 0.5 * (1.0 + lax.erf(value * (0.5**0.5)))
    pdf = jnp.exp(-0.5 * value * value) * ((2.0 * jnp.pi) ** -0.5)
    return value * cdf, cdf + value * pdf


def silu_grad(value):
    gate = jax.nn.sigmoid(value)
    return gate * (1.0 + value * (1.0 - gate))


def row_share(value, start, rows):
    return lax.dynamic_slice_in_dim(value, start, rows, 0)


def on_device(
    mp_size,
    dp_size,
    features,
    w_in,
    ln_gain,
    ln_bias,
    w_conv,
    se_down,
    se_down_bias,
    se_up,
    se_up_bias,
    w_out,
    w_read1,
    b_read1,
    w_read2,
    b_read2,
    out_grad,
    box_counts,
):
    images, side, _, width = features.shape
    half = side // 2
    local = w_in.shape[1]
    rows = (images * side * side, images * half * half)
    sides = (side, half)
    share = (rows[0] // mp_size, rows[1] // mp_size)
    mp = lax.axis_index("mp")

    def ex(name, collective, *pairs):
        return exchange(name, collective, mp_size, *pairs)

    feats = features.reshape(rows[0], width)
    grad_top = (
        out_grad.astype(f32) * box_counts.astype(f32)[:, None, None, None]
    ).astype(bf16).reshape(rows[1], -1)
    grad_b_read2 = jnp.sum(grad_top.astype(f32), axis=0)
    weights, vectors = gather_weights(
        mp_size,
        jnp.stack([w_in[0], w_out[0], w_in[1], w_out[1]]),
        jnp.concatenate([ln_gain, ln_bias], axis=0),
    )
    (grad_full,) = ex("gather_dout", 3, ("ag", grad_top))
    wide_in = (weights[0], weights[2])
    wide_out = (weights[1], weights[3])
    vectors = jnp.swapaxes(vectors, 0, 1).reshape(4, width)
    gains, shifts = vectors[:2], vectors[2:]

    def forward(index, low):
        h = nt(low, wide_in[index])
        normed, inv_std = normalize(h)
        norm = (normed * gains[index] + shifts[index]).astype(bf16)
        conv = conv_forward(norm, w_conv[index], images, sides[index])
        act = jax.nn.silu(conv)
        pooled = jnp.mean(act, axis=1)
        (pre_down,) = ex(
            "squeeze", 4 + index, ("psum", exact(pooled, se_down[index].astype(f32)))
        )
        pre_down = pre_down + se_down_bias[index]
        squeeze = jax.nn.silu(pre_down)
        excite = jax.nn.sigmoid(exact(squeeze, se_up[index].astype(f32)) + se_up_bias[index])
        scaled = act * excite[:, None, :]
        own_h = row_share(h, mp * share[index], share[index])
        return norm, conv, act, pooled, pre_down, squeeze, excite, scaled, own_h

    first = forward(0, feats)
    mean_scaled = pool(first[7].reshape(rows[0], -1), images, side).astype(bf16)
    (mean_scaled,) = ex("gather_scaled0", 6, ("ag", mean_scaled))
    mean_scaled = blocks_to_wide(mean_scaled)
    value = pool(feats, images, side) + nt(mean_scaled, wide_out[0])
    value_low = value.astype(bf16)
    second = forward(1, value_low)
    (scaled1,) = ex("gather_scaled1", 7, ("ag", second[7].reshape(rows[1], -1).astype(bf16)))
    scaled1 = blocks_to_wide(scaled1)
    top = (value + nt(scaled1, wide_out[1])).astype(bf16)
    act_full, slope = gelu_parts(nn(top, w_read1) + b_read1)
    act_low = act_full.astype(bf16)
    grad_full = blocks_to_wide(grad_full)
    grad_pre = (nt(grad_full, w_read2) * slope).astype(bf16)
    grad_b_read1 = jnp.sum(grad_pre.astype(f32), axis=0)
    (grad_out,) = ex(
        "scatter_g", 8, ("rs", nt(grad_pre, w_read1).astype(bf16).reshape(mp_size, share[1], width))
    )
    (readout,) = ex(
        "scatter_readout", 9, ("rs", wide_to_blocks(nn(act_low, w_read2).astype(bf16), mp_size))
    )
    readout = (readout + b_read2).astype(bf16).reshape(images, half, half, -1)
    grad_w_read2 = tn(act_low, grad_full)
    grad_w_read1 = tn(top, grad_pre)

    def to_channels(name, collective, *values):
        stacked = jnp.concatenate([wide_to_blocks(value, mp_size) for value in values], axis=1)
        (result,) = ex(name, collective, ("a2a", stacked))
        parts, start = [], 0
        for value in values:
            part = result[:, start : start + value.shape[0]]
            start += value.shape[0]
            parts.append(part)
        return parts

    def backward(index, grad_scaled, saved):
        norm, conv, act, pooled, pre_down, squeeze, excite, scaled, own_h = saved
        here = sides[index]
        gate_grad = jnp.sum(grad_scaled * act, axis=1)
        grad_up = gate_grad * excite * (1.0 - excite)
        (grad_squeeze,) = ex(
            "squeeze_back", 10 + index, ("psum", exact(grad_up, se_up[index].astype(f32).T))
        )
        grad_down = grad_squeeze * silu_grad(pre_down)
        grad_pooled = exact(grad_down, se_down[index].astype(f32).T)
        grad_act = grad_scaled * excite[:, None, :] + grad_pooled[:, None, :] / (here * here)
        grad_conv = (grad_act * silu_grad(conv)).astype(bf16).reshape(rows[index], -1)
        taps = shifted(grad_conv, images, here)
        grad_w_conv = tn(taps, norm).reshape(9, local, width)
        taps_weight = jnp.swapaxes(w_conv[index], 0, 1).reshape(9 * local, width)
        partial_norm = nn(taps, taps_weight).astype(bf16)
        (grad_norm,) = ex(
            "scatter_norm", 12 + index, ("rs", partial_norm.reshape(mp_size, share[index], width))
        )
        normed, inv_std = normalize(own_h)
        grad_gain = jnp.sum(grad_norm * normed, axis=0)
        grad_shift = jnp.sum(grad_norm, axis=0)
        scaled_grad = grad_norm * gains[index]
        grad_h = (
            inv_std
            * (
                scaled_grad
                - jnp.mean(scaled_grad, axis=1, keepdims=True)
                - normed * jnp.mean(scaled_grad * normed, axis=1, keepdims=True)
            )
        ).astype(bf16)
        small = (
            exact(squeeze.T, grad_up),
            jnp.sum(grad_up, axis=0),
            exact(pooled.T, grad_down),
            jnp.sum(grad_down, axis=0),
        )
        return grad_w_conv, grad_h, jnp.stack([grad_gain, grad_shift]), small

    grad_low = grad_out.astype(bf16)
    gs1, gy1 = to_channels("spread1", 14, nn(grad_low, wide_out[1]).astype(bf16), grad_low)
    gs1 = gs1.astype(f32).reshape(images, half * half, local)
    grad_w_out1 = tn(gy1.reshape(rows[1], local), scaled1)
    grad_w_conv1, grad_h1, lines1, small1 = backward(1, gs1, second)
    grad_value = (grad_out + nn(grad_h1, wide_in[1])) * 0.25
    grad_value_low = grad_value.astype(bf16)
    gs0, gy0, gh1 = to_channels(
        "spread0", 15, nn(grad_value_low, wide_out[0]).astype(bf16), grad_value_low, grad_h1
    )
    grad_w_in1 = tn(gh1.reshape(rows[1], local), value_low)
    grad_w_out0 = 4.0 * tn(gy0.reshape(rows[1], local), mean_scaled)
    residual = spread(gy0.astype(f32).reshape(rows[1], local), images, half)
    gs0 = spread(gs0.astype(f32).reshape(rows[1], local), images, half)
    grad_w_conv0, grad_h0, lines0, small0 = backward(
        0, gs0.reshape(images, side * side, local), first
    )
    grad_in = nn(grad_h0, wide_in[0]).astype(bf16)
    lines = jnp.concatenate([lines0, lines1], axis=0)
    stacked = jnp.concatenate(
        [wide_to_blocks(grad_in, mp_size), wide_to_blocks(grad_h0, mp_size)], axis=1
    )
    spread_all, lines = ex(
        "spread_last", 16, ("a2a", stacked), ("rs", wide_to_blocks(lines, mp_size))
    )
    grad_features = spread_all[:, : share[0]].astype(f32).reshape(rows[0], local) + residual
    grad_features = grad_features.reshape(images, side, side, local)
    grad_w_in0 = tn(spread_all[:, share[0] :].reshape(rows[0], local), feats)

    def parted(value, axis):
        shape = value.shape
        split = value.reshape(shape[:axis] + (dp_size, shape[axis] // dp_size) + shape[axis + 1 :])
        return jnp.moveaxis(split, axis, 0)

    scattered = dp_scatter(
        dp_size,
        [
            parted(jnp.stack([grad_w_in0, grad_w_in1]).astype(bf16), 2),
            parted(jnp.stack([grad_w_conv0, grad_w_conv1]).astype(bf16), 3),
            parted(jnp.stack([small0[2], small1[2]]).astype(bf16), 2),
            parted(jnp.stack([small0[0], small1[0]]).astype(bf16), 1),
            parted(jnp.stack([grad_w_out0, grad_w_out1]).astype(bf16), 2),
            parted(grad_w_read1.astype(bf16), 0),
            parted(grad_w_read2.astype(bf16), 1),
        ],
    )
    vectors = lax.psum(
        (
            lines[0::2],
            lines[1::2],
            jnp.stack([small0[3], small1[3]]),
            jnp.stack([small0[1], small1[1]]),
            grad_b_read1,
            grad_b_read2,
        ),
        "dp",
    )
    return (
        readout,
        grad_features,
        scattered[0],
        vectors[0],
        vectors[1],
        jnp.swapaxes(scattered[1], 1, 2),
        scattered[2],
        vectors[2],
        scattered[3],
        vectors[3],
        scattered[4],
        scattered[5],
        vectors[4],
        scattered[6],
        vectors[5],
    )


def solution(mesh):
    in_specs = (
        P("dp", None, None, None),
        P(None, "mp", None),
        P(None, "mp"),
        P(None, "mp"),
        P(None, "mp", None, None),
        P(None, "mp", None),
        P(),
        P(None, None, "mp"),
        P(None, "mp"),
        P(None, "mp", None),
        P(None, "mp"),
        P("mp"),
        P("mp", None),
        P("mp"),
        P("dp", None, None, "mp"),
        P("dp"),
    )
    out_specs = (
        P("dp", None, None, "mp"),
        P("dp", None, None, "mp"),
        P(None, "mp", "dp"),
        P(None, "mp"),
        P(None, "mp"),
        P(None, "mp", None, "dp"),
        P(None, "mp", "dp"),
        P(),
        P(None, "dp", "mp"),
        P(None, "mp"),
        P(None, "mp", "dp"),
        P("dp", "mp"),
        P("mp"),
        P("mp", "dp"),
        P("mp"),
    )
    body = partial(on_device, mesh.shape["mp"], mesh.shape["dp"])
    return jax.shard_map(
        body, mesh=mesh, in_specs=in_specs, out_specs=out_specs, check_vma=False
    )
```

```python
import math
from functools import partial

import jax
import jax.numpy as jnp
import numpy as np
from jax import lax
from jax.experimental import pallas as pl
from jax.experimental.pallas import tpu as pltpu
from jax.sharding import PartitionSpec as P

epsilon = 1e-06
highest = lax.Precision.HIGHEST
f32 = jnp.float32
bf16 = jnp.bfloat16
MESH = pl.DeviceIdType.MESH
VMEM_LIMIT = 56 << 20


def vmem_specs(count):
    return [pl.BlockSpec(memory_space=pltpu.VMEM)] * count


def barrier(peers):
    sem = pltpu.get_barrier_semaphore()
    for peer in peers:
        pl.semaphore_signal(sem, inc=1, device_id=peer, device_id_type=MESH)
    pl.semaphore_wait(sem, len(peers))


def sent(src, dst, send_sem, recv_sem, peer):
    return pltpu.make_async_remote_copy(
        src_ref=src,
        dst_ref=dst,
        send_sem=send_sem,
        recv_sem=recv_sem,
        device_id=peer,
        device_id_type=MESH,
    )


def exchange_kernel(size, kinds, *refs):
    count = len(kinds)
    sources, results = refs[:count], refs[count : 2 * count]
    slots = list(refs[2 * count : -2])
    send_sem, recv_sem = refs[-2:]
    landing = [slots.pop(0) if kind in ("rs", "psum") else result for kind, result in zip(kinds, results)]
    dp, mp = lax.axis_index("dp"), lax.axis_index("mp")
    peers = [(dp, lax.rem(mp + step, size)) for step in range(1, size)]
    barrier(peers)
    copies = []
    for index, kind in enumerate(kinds):
        for step, peer in enumerate(peers):
            src = sources[index].at[peer[1]] if kind in ("rs", "a2a") else sources[index]
            copy = sent(
                src, landing[index].at[mp], send_sem.at[index, step], recv_sem.at[index, step], peer
            )
            copy.start()
            copies.append(copy)
    for index, kind in enumerate(kinds):
        if kind in ("rs", "a2a"):
            landing[index][mp] = sources[index][mp]
        else:
            landing[index][mp] = sources[index][...]
    for copy in copies:
        copy.wait()
    for index, kind in enumerate(kinds):
        if kind in ("rs", "psum"):
            total = landing[index][0].astype(f32)
            for step in range(1, size):
                total = total + landing[index][step].astype(f32)
            results[index][...] = total


def exchange(name, collective, size, *pairs):
    kinds = tuple(kind for kind, value in pairs)
    values = [value for kind, value in pairs]
    shapes, scratch = [], []
    for kind, value in pairs:
        block = value.shape[1:] if kind in ("rs", "a2a") else value.shape
        if kind in ("rs", "psum"):
            shapes.append(jax.ShapeDtypeStruct(block, f32))
            scratch.append(pltpu.VMEM((size,) + block, value.dtype))
        else:
            shapes.append(jax.ShapeDtypeStruct((size,) + block, value.dtype))
    sems = pltpu.SemaphoreType.DMA((len(pairs), size - 1))
    return pl.pallas_call(
        partial(exchange_kernel, size, kinds),
        name=name,
        out_shape=shapes,
        in_specs=vmem_specs(len(values)),
        out_specs=vmem_specs(len(values)),
        scratch_shapes=scratch + [sems, sems],
        compiler_params=pltpu.CompilerParams(
            collective_id=collective, has_side_effects=True, vmem_limit_bytes=VMEM_LIMIT
        ),
    )(*values)


def weights_kernel(size, w_ref, gb_ref, out_ref, gb_out, ss, rs, cs, cr, gs, gr):
    dp, mp = lax.axis_index("dp"), lax.axis_index("mp")
    core = lax.rem(dp, 2)
    sibling = (dp + 1 - 2 * core, mp)
    peers = [(dp, lax.rem(mp + step, size)) for step in range(1, size)]
    barrier(peers + [sibling])
    count, rows = w_ref.shape[0], w_ref.shape[1]
    half = rows // 2
    mine = pl.ds(pl.multiple_of(core * half, half), half)

    def part(owner):
        return pl.ds(pl.multiple_of(owner * rows + core * half, half), half)

    copies = []
    for step, peer in enumerate(peers):
        copy = sent(gb_ref, gb_out.at[mp], gs.at[step], gr.at[step], peer)
        copy.start()
        copies.append(copy)
    outgoing = {}
    for which in range(count):
        for step, peer in enumerate(peers):
            copy = sent(
                w_ref.at[which, mine],
                out_ref.at[which, part(mp)],
                ss.at[which, step],
                rs.at[which, step],
                peer,
            )
            copy.start()
            outgoing[which, step] = copy
    gb_out[mp] = gb_ref[...]
    for which in range(count):
        out_ref[which, pl.ds(pl.multiple_of(mp * rows, rows), rows), :] = w_ref[which]
    for which in range(count):
        for step in range(size - 1):
            owner = lax.rem(mp + size - 1 - step, size)
            outgoing[which, step].wait_recv()
            copy = sent(
                out_ref.at[which, part(owner)],
                out_ref.at[which, part(owner)],
                cs.at[which, step],
                cr.at[which, step],
                sibling,
            )
            copy.start()
            copies.append(copy)
    for copy in outgoing.values():
        copy.wait_send()
    for copy in copies:
        copy.wait()


def gather_weights(size, weights, vectors):
    count, rows, width = weights.shape
    sem = pltpu.SemaphoreType.DMA((count, size - 1))
    vector_sem = pltpu.SemaphoreType.DMA((size - 1,))
    return pl.pallas_call(
        partial(weights_kernel, size),
        name="gather_weights",
        out_shape=[
            jax.ShapeDtypeStruct((count, rows * size, width), weights.dtype),
            jax.ShapeDtypeStruct((size,) + vectors.shape, vectors.dtype),
        ],
        in_specs=vmem_specs(2),
        out_specs=vmem_specs(2),
        scratch_shapes=[sem, sem, sem, sem, vector_sem, vector_sem],
        compiler_params=pltpu.CompilerParams(
            collective_id=1, has_side_effects=True, vmem_limit_bytes=VMEM_LIMIT
        ),
    )(weights, vectors)


def dp_kernel(size, *refs):
    count = (len(refs) - 4) // 4
    sources = refs[:count]
    results = refs[count : 2 * count]
    first = refs[2 * count : 3 * count]
    second = refs[3 * count : 4 * count]
    cs, cr, ys, yr = refs[4 * count :]
    dp, mp = lax.axis_index("dp"), lax.axis_index("mp")
    core = lax.rem(dp, 2)
    y = lax.div(dp, 2)
    chips = size // 2
    sibling = (dp + 1 - 2 * core, mp)
    others = [(2 * lax.rem(y + step, chips) + core, mp) for step in range(1, chips)]
    barrier([sibling] + others)
    copies = []
    for index in range(count):
        for chip in range(chips):
            copy = sent(
                sources[index].at[2 * chip + 1 - core],
                first[index].at[chip],
                cs.at[index, chip],
                cr.at[index, chip],
                sibling,
            )
            copy.start()
            copies.append(copy)
    late = []
    for index in range(count):
        for chip in range(chips):
            copies[index * chips + chip].wait_recv()
            first[index][chip] = (
                first[index][chip].astype(f32) + sources[index][2 * chip + core].astype(f32)
            ).astype(first[index].dtype)
        for step, peer in enumerate(others):
            copy = sent(
                first[index].at[lax.rem(y + step + 1, chips)],
                second[index].at[step],
                ys.at[index, step],
                yr.at[index, step],
                peer,
            )
            copy.start()
            late.append((index, copy))
    for index in range(count):
        total = first[index][y].astype(f32)
        for step in range(chips - 1):
            late[index * (chips - 1) + step][1].wait_recv()
            total = total + second[index][step].astype(f32)
        results[index][...] = total
    for copy in copies:
        copy.wait_send()
    for index, copy in late:
        copy.wait_send()


def dp_scatter(size, values):
    count, chips = len(values), size // 2
    first = [pltpu.VMEM((chips,) + value.shape[1:], value.dtype) for value in values]
    second = [pltpu.VMEM((max(chips - 1, 1),) + value.shape[1:], value.dtype) for value in values]
    core_sem = pltpu.SemaphoreType.DMA((count, chips))
    y_sem = pltpu.SemaphoreType.DMA((count, max(chips - 1, 1)))
    return pl.pallas_call(
        partial(dp_kernel, size),
        name="dp_scatter",
        out_shape=[jax.ShapeDtypeStruct(value.shape[1:], f32) for value in values],
        in_specs=vmem_specs(count),
        out_specs=vmem_specs(count),
        scratch_shapes=first + second + [core_sem, core_sem, y_sem, y_sem],
        compiler_params=pltpu.CompilerParams(
            collective_id=2, has_side_effects=True, vmem_limit_bytes=VMEM_LIMIT
        ),
    )(*values)


def nt(left, right):
    return lax.dot_general(left, right, (((1,), (1,)), ((), ())), preferred_element_type=f32)


def nn(left, right):
    return lax.dot_general(left, right, (((1,), (0,)), ((), ())), preferred_element_type=f32)


def tn(left, right):
    return lax.dot_general(left, right, (((0,), (0,)), ((), ())), preferred_element_type=f32)


def exact(left, right):
    return jnp.dot(left, right, precision=highest)


def blocks_to_wide(value):
    return jnp.swapaxes(value, 0, 1).reshape(value.shape[1], -1)


def wide_to_blocks(value, count):
    return jnp.swapaxes(value.reshape(value.shape[0], count, -1), 0, 1)


def normalize(h):
    mean = jnp.mean(h, axis=1, keepdims=True)
    centered = h - mean
    inv_std = lax.rsqrt(jnp.mean(centered * centered, axis=1, keepdims=True) + epsilon)
    return centered * inv_std, inv_std


def conv_forward(norm, w_conv, images, side):
    width = norm.shape[1]
    out = lax.conv_general_dilated(
        norm.reshape(images, side, side, width),
        w_conv.reshape(w_conv.shape[0], 3, 3, width),
        (1, 1),
        ((1, 1), (1, 1)),
        dimension_numbers=("NHWC", "OHWI", "NHWC"),
        preferred_element_type=f32,
    )
    return out.reshape(images, side * side, -1)


def shifted(grad_conv, images, side):
    width = grad_conv.shape[1]
    padded = jnp.pad(grad_conv.reshape(images, side, side, width), ((0, 0), (1, 1), (1, 1), (0, 0)))
    parts = [
        padded[:, 2 - tap // 3 : 2 - tap // 3 + side, 2 - tap % 3 : 2 - tap % 3 + side, :]
        for tap in range(9)
    ]
    return jnp.stack(parts, axis=3).reshape(images * side * side, 9 * width)


def pool(value, images, side):
    half = side // 2
    shape = (images, half, 2, half, 2, value.shape[-1])
    return jnp.mean(value.astype(f32).reshape(shape), axis=(2, 4)).reshape(images * half * half, -1)


def spread(value, images, half):
    grid = value.reshape(images, half, 1, half, 1, value.shape[-1])
    full = jnp.broadcast_to(grid, (images, half, 2, half, 2, value.shape[-1]))
    return full.reshape(images * 4 * half * half, -1)


def gelu_parts(value):
    cdf = 0.5 * (1.0 + lax.erf(value * (0.5**0.5)))
    pdf = jnp.exp(-0.5 * value * value) * ((2.0 * jnp.pi) ** -0.5)
    return value * cdf, cdf + value * pdf


def silu_grad(value):
    gate = jax.nn.sigmoid(value)
    return gate * (1.0 + value * (1.0 - gate))


def row_share(value, start, rows):
    return lax.dynamic_slice_in_dim(value, start, rows, 0)


def dot(left, right, left_dim, right_dim):
    return lax.dot_general(
        left, right, (((left_dim,), (right_dim,)), ((), ())), preferred_element_type=f32
    )


def exact_dot(left, right, left_dim=1, right_dim=0):
    return lax.dot_general(
        left,
        right,
        (((left_dim,), (right_dim,)), ((), ())),
        precision=highest,
        preferred_element_type=f32,
    )


class Place:
    def __init__(self):
        self.dp, self.mp = lax.axis_index("dp"), lax.axis_index("mp")
        self.z, self.x = lax.div(self.mp, 2), lax.rem(self.mp, 2)
        self.y, self.core = lax.div(self.dp, 2), lax.rem(self.dp, 2)
        self.other_x = 1 - self.x
        self.z_peers = {k: (self.dp, 2 * lax.rem(self.z + k, 4) + self.x) for k in (1, 3, 2)}
        self.z_from = {k: lax.rem(self.z + 4 - k, 4) for k in (0, 1, 3, 2)}
        self.x_peer = (self.dp, 2 * self.z + self.other_x)
        self.y_peer = (2 * (1 - self.y) + self.core, self.mp)
        self.core_peer = (2 * self.y + 1 - self.core, self.mp)
        self.mp_peers = {k: (self.dp, lax.rem(self.mp + k, 8)) for k in range(1, 8)}

    def greet(self):
        barrier(list(self.mp_peers.values()) + [self.y_peer, self.core_peer])


class Flight:
    def __init__(self):
        self.sends = []

    def remote(self, src, dst, send_sem, recv_sem, peer):
        copy = sent(src, dst, send_sem, recv_sem, peer)
        copy.start()
        self.sends.append(copy)
        return copy

    def drain(self):
        for copy in self.sends:
            copy.wait_send()
        self.sends = []


def gather_start(place, flight, buf, zs, zr, xs, xr):
    own = buf.at[place.z, place.x]
    first = {}
    for k, peer in place.z_peers.items():
        first[k] = flight.remote(own, own, zs.at[k], zr.at[k], peer)
    second = {0: flight.remote(own, own, xs.at[0], xr.at[0], place.x_peer)}
    return first, second


def gather_turn(place, flight, buf, xs, xr, first, second):
    for k in (1, 3, 2):
        first[k].wait_recv()
        block = buf.at[place.z_from[k], place.x]
        second[k] = flight.remote(block, block, xs.at[k], xr.at[k], place.x_peer)


def gather_end(second):
    for copy in second.values():
        copy.wait_recv()


def sum_small(place, flight, own, slots, ss, rs):
    copies = []
    for k, peer in place.mp_peers.items():
        copies.append(flight.remote(own, slots.at[k - 1], ss.at[k - 1], rs.at[k - 1], peer))
    total = own[...]
    for k, copy in enumerate(copies):
        copy.wait_recv()
        total = total + slots[k]
    return total


def normalize_rows(h_ref, norm_ref, gain, shift, rows, step):
    @pl.loop(0, rows // step)
    def _(index):
        part = pl.ds(pl.multiple_of(index * step, step), step)
        h = h_ref[part, :]
        mean = jnp.mean(h, axis=1, keepdims=True)
        centered = h - mean
        var = jnp.mean(centered * centered, axis=1, keepdims=True)
        norm_ref[part, :] = (centered * lax.rsqrt(var + epsilon) * gain + shift).astype(bf16)


def conv_grid(norm_ref, start, wc_ref, y_ref, side_ref, side, stride, masks):
    rows = side * stride
    for a in range(3):
        columns = pl.ds(a * 384, 384)
        y_ref[pl.ds(stride, rows), columns] = dot(
            norm_ref[pl.ds(start, rows), :], wc_ref[columns, :], 1, 1
        )
    sums = []
    for b in range(3):
        total = y_ref[pl.ds(0, rows), pl.ds(b * 128, 128)]
        total = total + y_ref[pl.ds(stride, rows), pl.ds(384 + b * 128, 128)]
        total = total + y_ref[pl.ds(2 * stride, rows), pl.ds(768 + b * 128, 128)]
        sums.append(total)
    side_ref[0, pl.ds(8, rows), :] = sums[0]
    side_ref[1, pl.ds(8, rows), :] = sums[2]
    left = side_ref[0, pl.ds(7, rows), :]
    right = side_ref[1, pl.ds(9, rows), :]
    if masks is not None:
        left, right = left * masks[0], right * masks[1]
    return sums[1] + left + right


def column_index(side, stride):
    shape = (side, stride, 128)
    return lax.broadcasted_iota(jnp.int32, shape, 1).reshape(side * stride, 128)


def edge_masks(side):
    column = column_index(side, side)
    return (column > 0).astype(f32), (column < side - 1).astype(f32)


def inner_mask(side, stride):
    return (column_index(side, stride) < side).astype(f32)


def forward_kernel(
    feats,
    w_in,
    w_out,
    wc,
    dout,
    w_read1,
    w_read2,
    lines,
    se_down,
    se_down_bias,
    se_up,
    se_up_bias,
    b_read1,
    pool_mat,
    wide_mat,
    slim_mat,
    pack_mat,
    unpack_mat,
    o_norm0,
    o_norm1,
    o_conv0,
    o_conv1,
    o_se,
    o_h0,
    o_h1,
    o_mean,
    o_scaled,
    o_value,
    o_top,
    o_act,
    o_dpre,
    o_g,
    o_w,
    o_lines,
    o_dout,
    v_feats,
    v_w,
    v_wc,
    v_read1,
    v_read2,
    v_dout,
    v_h,
    v_norm0,
    v_y,
    v_side,
    v_y1,
    v_side1,
    v_lines,
    v_conv0,
    v_act0,
    v_mean,
    v_wide,
    v_value,
    v_low,
    v_norm1,
    v_norm1e,
    v_conv1,
    v_scaled,
    v_top,
    v_act,
    v_slope,
    v_dpre,
    v_g,
    v_slots,
    v_small,
    v_se,
    load_sem,
    store_sem,
    wzs,
    wzr,
    wxs,
    wxr,
    wys,
    wyr,
    wcs,
    wcr,
    gzs,
    gzr,
    gxs,
    gxr,
    sms,
    smr,
):
    place = Place()
    flight = Flight()
    z, x, dp, mp = place.z, place.x, place.dp, place.mp
    quarter = w_in.shape[1] // 4
    own_rows = pl.ds(pl.multiple_of(dp * quarter, quarter), quarter)
    weights = (w_in.at[0], w_out.at[0], w_in.at[1], w_out.at[1])

    local = []

    def load(src, dst):
        copy = pltpu.make_async_copy(src, dst, load_sem.at[len(local)])
        copy.start()
        local.append(copy)
        return copy

    stores = []

    def store(src, dst):
        copy = pltpu.make_async_copy(src, dst, store_sem.at[len(stores)])
        copy.start()
        stores.append(copy)

    own_weights = [
        load(weights[which].at[own_rows], v_w.at[which, z, x, dp]) for which in range(4)
    ]
    own_dout = load(dout, v_dout.at[z, x])
    v_lines[z, x] = lines[...]
    got_feats = load(feats, v_feats)
    got_wc0 = load(wc.at[0], v_wc.at[0])
    got_read1 = load(w_read1, v_read1)
    got_read2 = load(w_read2, v_read2)
    got_wc1 = load(wc.at[1], v_wc.at[1])
    place.greet()

    line_flight = gather_start(place, flight, v_lines, gzs.at[0], gzr.at[0], gxs.at[0], gxr.at[0])
    own_weights[0].wait()

    def block(which, k, other, q):
        column = place.other_x if other else x
        return v_w.at[which, place.z_from[k], column, q]

    near, far = dp, 2 * (1 - place.y) + place.core
    first, second, third, fourth = {}, {}, {}, []

    def pass_core(k, other, q, slot):
        src = block(0, k, other, q)
        fourth.append(
            flight.remote(
                src, src, wcs.at[0, k, other, slot], wcr.at[0, k, other, slot], place.core_peer
            )
        )

    def pass_y(k, other):
        src = block(0, k, other, near)
        third[k, other] = flight.remote(
            src, src, wys.at[0, k, other], wyr.at[0, k, other], place.y_peer
        )
        pass_core(k, other, near, 0)

    def pass_x(k):
        src = block(0, k, 0, near)
        second[k] = flight.remote(src, src, wxs.at[0, k], wxr.at[0, k], place.x_peer)

    own = block(0, 0, 0, near)
    for k, peer in place.z_peers.items():
        first[k] = flight.remote(own, own, wzs.at[0, k], wzr.at[0, k], peer)
    pass_x(0)
    pass_y(0, 0)
    for k in (1, 3, 2):
        first[k].wait_recv()
        pass_x(k)
        pass_y(k, 0)
    bulk_z = {}
    for which in (1, 2, 3):
        own_weights[which].wait()
        own = v_w.at[which, z, x, dp]
        for k, peer in place.z_peers.items():
            bulk_z[which, k] = flight.remote(own, own, wzs.at[which, k], wzr.at[which, k], peer)
    for k in (0, 1, 3, 2):
        second[k].wait_recv()
        pass_y(k, 1)
    for other in (0, 1):
        for k in (0, 1, 3, 2):
            third[k, other].wait_recv()
            pass_core(k, other, far, 1)
    gather_turn(place, flight, v_lines, gxs.at[0], gxr.at[0], *line_flight)
    own_dout.wait()
    dout_flight = gather_start(place, flight, v_dout, gzs.at[1], gzr.at[1], gxs.at[1], gxr.at[1])

    images = 2
    grid0, grid1, conv1_rows = v_feats.shape[0] // images, v_low.shape[0] // images, v_norm1e.shape[0] // images
    side0 = 24
    got_feats.wait()
    for image in range(images):
        v_value[pl.ds(image * grid1, grid1), :] = dot(
            pool_mat[...], v_feats[pl.ds(image * grid0, grid0), :], 1, 0
        )
    v_y[...] = jnp.zeros_like(v_y)
    v_y1[...] = jnp.zeros_like(v_y1)
    v_side[...] = jnp.zeros_like(v_side)
    v_side1[...] = jnp.zeros_like(v_side1)
    gather_end(line_flight[1])
    line = jnp.concatenate([v_lines[a, b] for a in range(4) for b in range(2)], axis=1)
    store(v_lines, o_lines)

    for copy in fourth:
        copy.wait_recv()

    def wide_weight(which, index):
        return v_w[which, index].reshape(2 * 4 * quarter, v_w.shape[-1])

    def bulk_x():
        copies = []
        for which in (1, 2, 3):
            for k in (1, 3, 2):
                bulk_z[which, k].wait_recv()
            src = v_w.at[which, :, x, near]
            copies.append(
                flight.remote(src, src, wxs.at[which, 0], wxr.at[which, 0], place.x_peer)
            )
        return copies

    def bulk_y(copies):
        result = []
        for which, copy in zip((1, 2, 3), copies):
            copy.wait_recv()
            src = v_w.at[which, :, :, near]
            result.append(
                flight.remote(src, src, wys.at[which, 0, 0], wyr.at[which, 0, 0], place.y_peer)
            )
        return result

    def bulk_core(copies):
        result = []
        for which, copy in zip((1, 2, 3), copies):
            copy.wait_recv()
            for slot, q in enumerate((near, far)):
                src = v_w.at[which, :, :, q]
                result.append(
                    flight.remote(
                        src,
                        src,
                        wcs.at[which, 0, 0, slot],
                        wcr.at[which, 0, 0, slot],
                        place.core_peer,
                    )
                )
        return result

    bulk = bulk_x()

    @pl.loop(0, 4)
    def _(index):
        columns = pl.ds(pl.multiple_of(index * 256, 256), 256)
        v_h[:, columns] = dot(v_feats[...], wide_weight(0, index), 1, 1)

    share0 = v_h.shape[0] // 8
    store(v_h.at[pl.ds(pl.multiple_of(mp * share0, share0), share0)], o_h0)
    bulk = bulk_y(bulk)
    normalize_rows(v_h, v_norm0, line[0:1], line[2:3], v_h.shape[0], 32)
    store(v_norm0, o_norm0)
    got_wc0.wait()
    masks = edge_masks(side0)
    pooled = []
    for image in range(images):
        conv = conv_grid(
            v_norm0, image * grid0, v_wc.at[0], v_y, v_side, side0, side0, masks
        )
        v_conv0[pl.ds(image * grid0, grid0), :] = conv
        act = conv * jax.nn.sigmoid(conv)
        v_act0[pl.ds(image * grid0, grid0), :] = act
        pooled.append(jnp.sum(act, axis=0, keepdims=True) * (1.0 / grid0))
    store(v_conv0, o_conv0)
    gather_turn(place, flight, v_dout, gxs.at[1], gxr.at[1], *dout_flight)

    def excite(index, pooled):
        pooled = jnp.concatenate(pooled + [jnp.zeros((6, 128), f32)], axis=0)
        v_small[index] = exact_dot(pooled, se_down[index].astype(f32))
        pre = sum_small(
            place, flight, v_small.at[index], v_slots.at[index], sms.at[index], smr.at[index]
        )
        pre = pre + se_down_bias[index : index + 1, :]
        squeeze = pre * jax.nn.sigmoid(pre)
        gate = jax.nn.sigmoid(
            exact_dot(squeeze, se_up[index].astype(f32)) + se_up_bias[index : index + 1, :]
        )
        v_se[index, :, 0:128] = pooled
        v_se[index, :, 128:256] = gate
        v_se[index, :, 256:512] = pre
        return gate

    gate = excite(0, pooled)
    for image in range(images):
        scaled = (v_act0[pl.ds(image * grid0, grid0), :] * gate[image : image + 1, :]).astype(bf16)
        v_mean[z, x, pl.ds(image * grid1, grid1), :] = dot(pool_mat[...], scaled, 1, 0).astype(bf16)
    flying = gather_start(place, flight, v_mean, gzs.at[2], gzr.at[2], gxs.at[2], gxr.at[2])
    gather_turn(place, flight, v_mean, gxs.at[2], gxr.at[2], *flying)
    bulk = bulk_core(bulk)
    gather_end(flying[1])
    store(v_mean, o_mean)
    for copy in bulk:
        copy.wait_recv()
    store(v_w, o_w)

    def widen(src):
        for a in range(4):
            for b in range(2):
                v_wide[:, pl.ds((2 * a + b) * 128, 128)] = src[a, b]

    widen(v_mean)
    for index in range(4):
        columns = pl.ds(index * 256, 256)
        value = v_value[:, columns] + dot(v_wide[...], wide_weight(1, index), 1, 1)
        v_value[:, columns] = value
        v_low[:, columns] = value.astype(bf16)
    store(v_low, o_value)
    rows1 = v_low.shape[0]
    share1 = rows1 // 8
    h1 = v_h.at[pl.ds(0, rows1)]
    stores[1].wait()
    for index in range(4):
        h1[:, pl.ds(index * 256, 256)] = dot(v_low[...], wide_weight(2, index), 1, 1)
    store(h1.at[pl.ds(pl.multiple_of(mp * share1, share1), share1)], o_h1)
    normalize_rows(h1, v_norm1, line[1:2], line[3:4], rows1, 32)
    for image in range(images):
        v_norm1e[pl.ds(image * conv1_rows, conv1_rows), :] = dot(
            wide_mat[...], v_norm1[pl.ds(image * grid1, grid1), :], 1, 0
        ).astype(bf16)
    store(v_norm1e, o_norm1)
    got_wc1.wait()
    inner = inner_mask(12, 16)
    acts, pooled = [], []
    for image in range(images):
        conv = conv_grid(
            v_norm1e, image * conv1_rows, v_wc.at[1], v_y1, v_side1, 12, 16, None
        )
        v_conv1[pl.ds(image * conv1_rows, conv1_rows), :] = conv
        act = conv * jax.nn.sigmoid(conv) * inner
        acts.append(act)
        pooled.append(jnp.sum(act, axis=0, keepdims=True) * (1.0 / 144))
    store(v_conv1, o_conv1)
    gate = excite(1, pooled)
    store(v_se, o_se)
    for image in range(images):
        scaled = (acts[image] * gate[image : image + 1, :]).astype(bf16)
        v_scaled[z, x, pl.ds(image * grid1, grid1), :] = dot(slim_mat[...], scaled, 1, 0).astype(bf16)
    flying = gather_start(place, flight, v_scaled, gzs.at[3], gzr.at[3], gxs.at[3], gxr.at[3])
    gather_turn(place, flight, v_scaled, gxs.at[3], gxr.at[3], *flying)
    gather_end(flying[1])
    store(v_scaled, o_scaled)
    widen(v_scaled)
    slim_rows = v_top.shape[0] // images
    for index in range(4):
        columns = pl.ds(index * 256, 256)
        value = v_value[:, columns] + dot(v_wide[...], wide_weight(3, index), 1, 1)
        value = value.astype(bf16)
        for image in range(images):
            v_top[pl.ds(image * slim_rows, slim_rows), columns] = dot(
                pack_mat[...], value[image * grid1 : (image + 1) * grid1, :], 1, 0
            ).astype(bf16)
    store(v_top, o_top)

    got_read1.wait()
    for index in range(v_act.shape[1] // 256):
        columns = pl.ds(index * 256, 256)
        pre = dot(v_top[...], v_read1[:, columns], 1, 0) + b_read1[:, columns]
        cdf = 0.5 * (1.0 + lax.erf(pre * (0.5**0.5)))
        v_act[:, columns] = (pre * cdf).astype(bf16)
        v_slope[:, columns] = cdf + pre * (jnp.exp(-0.5 * pre * pre) * (2.0 * math.pi) ** -0.5)
    store(v_act, o_act)
    got_read2.wait()
    gather_end(dout_flight[1])
    store(v_dout, o_dout)
    width = v_dout.shape[-1]
    for part in range(2):
        hidden = pl.ds(part * 256, 256)
        total = jnp.zeros((v_top.shape[0], 256), f32)
        for a in range(4):
            for b in range(2):
                total = total + dot(
                    v_dout[a, b], v_read2[hidden, pl.ds((2 * a + b) * width, width)], 1, 1
                )
        v_dpre[:, hidden] = (total * v_slope[:, hidden]).astype(bf16)
    store(v_dpre, o_dpre)
    wide_dpre = jnp.concatenate(
        [
            dot(unpack_mat[...], v_dpre[pl.ds(image * slim_rows, slim_rows), :], 1, 0).astype(bf16)
            for image in range(images)
        ],
        axis=0,
    )
    for index in range(4):
        columns = pl.ds(index * 256, 256)
        part = dot(wide_dpre, v_read1[columns, :], 1, 1)
        for owner in range(8):
            v_g[owner, :, columns] = part[owner * share1 : (owner + 1) * share1, :].astype(bf16)
    store(v_g, o_g)
    flight.drain()
    for index, copy in enumerate(stores):
        if index != 1:
            copy.wait()


def selections():
    pool_mat = np.zeros((160, 576), np.float32)
    wide_mat = np.zeros((192, 160), np.float32)
    pack_mat = np.zeros((144, 160), np.float32)
    for row in range(12):
        for column in range(12):
            padded = 40 * (row // 3) + 12 * (row % 3) + column
            wide_mat[16 * row + column, padded] = 1.0
            pack_mat[12 * row + column, padded] = 1.0
            for down in range(2):
                for right in range(2):
                    pool_mat[padded, 24 * (2 * row + down) + 2 * column + right] = 0.25
    return [
        jnp.asarray(mat, bf16) for mat in (pool_mat, wide_mat, wide_mat.T, pack_mat, pack_mat.T)
    ]


def run_forward(feats, w_in, w_out, wc, dout, w_read1, w_read2, lines, smalls, mats):
    def shaped(dtype, *dims):
        return jax.ShapeDtypeStruct(dims, dtype)

    outs = [
        shaped(bf16, 1152, 1024),
        shaped(bf16, 384, 1024),
        shaped(f32, 1152, 128),
        shaped(f32, 384, 128),
        shaped(f32, 2, 8, 512),
        shaped(f32, 144, 1024),
        shaped(f32, 40, 1024),
        shaped(bf16, 4, 2, 320, 128),
        shaped(bf16, 4, 2, 320, 128),
        shaped(bf16, 320, 1024),
        shaped(bf16, 288, 1024),
        shaped(bf16, 288, 512),
        shaped(bf16, 288, 512),
        shaped(bf16, 8, 40, 1024),
        shaped(bf16, 4, 4, 2, 4, 32, 1024),
        shaped(f32, 4, 2, 4, 128),
        shaped(bf16, 4, 2, 288, 512),
    ]
    scratch = [
        (bf16, 1152, 1024),
        (bf16, 4, 4, 2, 4, 32, 1024),
        (bf16, 2, 1152, 1024),
        (bf16, 1024, 512),
        (bf16, 512, 4096),
        (bf16, 4, 2, 288, 512),
        (f32, 1152, 1024),
        (bf16, 1152, 1024),
        (f32, 624, 1152),
        (f32, 2, 592, 128),
        (f32, 224, 1152),
        (f32, 2, 208, 128),
        (f32, 4, 2, 4, 128),
        (f32, 1152, 128),
        (f32, 1152, 128),
        (bf16, 4, 2, 320, 128),
        (bf16, 320, 1024),
        (f32, 320, 1024),
        (bf16, 320, 1024),
        (bf16, 320, 1024),
        (bf16, 384, 1024),
        (f32, 384, 128),
        (bf16, 4, 2, 320, 128),
        (bf16, 288, 1024),
        (bf16, 288, 512),
        (f32, 288, 512),
        (bf16, 288, 512),
        (bf16, 8, 40, 1024),
        (f32, 2, 7, 8, 256),
        (f32, 2, 8, 256),
        (f32, 2, 8, 512),
    ]
    dma = pltpu.SemaphoreType.DMA
    sems = [(12,), (20,), (4, 4), (4, 4), (4, 4), (4, 4), (4, 4, 2), (4, 4, 2)]
    sems += [(4, 4, 2, 2), (4, 4, 2, 2), (4, 4), (4, 4), (4, 4), (4, 4), (2, 7), (2, 7)]
    anywhere = [pl.BlockSpec(memory_space=pl.ANY)]
    operands = [feats, w_in, w_out, wc, dout, w_read1, w_read2]
    return pl.pallas_call(
        forward_kernel,
        name="forward",
        out_shape=outs,
        in_specs=anywhere * len(operands) + vmem_specs(1 + len(smalls) + len(mats)),
        out_specs=anywhere * len(outs),
        scratch_shapes=[pltpu.VMEM(dims, dtype) for dtype, *dims in scratch]
        + [dma(shape) for shape in sems],
        compiler_params=pltpu.CompilerParams(
            collective_id=20, has_side_effects=True, vmem_limit_bytes=60 << 20
        ),
    )(*operands, lines, *smalls, *mats)


def on_device(
    mp_size,
    dp_size,
    features,
    w_in,
    ln_gain,
    ln_bias,
    w_conv,
    se_down,
    se_down_bias,
    se_up,
    se_up_bias,
    w_out,
    w_read1,
    b_read1,
    w_read2,
    b_read2,
    out_grad,
    box_counts,
):
    images, side, _, width = features.shape
    half = side // 2
    local = w_in.shape[1]
    rows = (images * side * side, images * half * half)
    sides = (side, half)
    share = (rows[0] // mp_size, rows[1] // mp_size)
    mp = lax.axis_index("mp")

    def ex(name, collective, *pairs):
        return exchange(name, collective, mp_size, *pairs)

    feats = features.reshape(rows[0], width)
    grad_top = (
        out_grad.astype(f32) * box_counts.astype(f32)[:, None, None, None]
    ).astype(bf16).reshape(rows[1], -1)
    grad_b_read2 = jnp.sum(grad_top.astype(f32), axis=0)
    weights, vectors = gather_weights(
        mp_size,
        jnp.stack([w_in[0], w_out[0], w_in[1], w_out[1]]),
        jnp.concatenate([ln_gain, ln_bias], axis=0),
    )
    (grad_full,) = ex("gather_dout", 3, ("ag", grad_top))
    wide_in = (weights[0], weights[2])
    wide_out = (weights[1], weights[3])
    vectors = jnp.swapaxes(vectors, 0, 1).reshape(4, width)
    gains, shifts = vectors[:2], vectors[2:]

    def forward(index, low):
        h = nt(low, wide_in[index])
        normed, inv_std = normalize(h)
        norm = (normed * gains[index] + shifts[index]).astype(bf16)
        conv = conv_forward(norm, w_conv[index], images, sides[index])
        act = jax.nn.silu(conv)
        pooled = jnp.mean(act, axis=1)
        (pre_down,) = ex(
            "squeeze", 4 + index, ("psum", exact(pooled, se_down[index].astype(f32)))
        )
        pre_down = pre_down + se_down_bias[index]
        squeeze = jax.nn.silu(pre_down)
        excite = jax.nn.sigmoid(exact(squeeze, se_up[index].astype(f32)) + se_up_bias[index])
        scaled = act * excite[:, None, :]
        own_h = row_share(h, mp * share[index], share[index])
        return norm, conv, act, pooled, pre_down, squeeze, excite, scaled, own_h

    first = forward(0, feats)
    mean_scaled = pool(first[7].reshape(rows[0], -1), images, side).astype(bf16)
    (mean_scaled,) = ex("gather_scaled0", 6, ("ag", mean_scaled))
    mean_scaled = blocks_to_wide(mean_scaled)
    value = pool(feats, images, side) + nt(mean_scaled, wide_out[0])
    value_low = value.astype(bf16)
    second = forward(1, value_low)
    (scaled1,) = ex("gather_scaled1", 7, ("ag", second[7].reshape(rows[1], -1).astype(bf16)))
    scaled1 = blocks_to_wide(scaled1)
    top = (value + nt(scaled1, wide_out[1])).astype(bf16)
    act_full, slope = gelu_parts(nn(top, w_read1) + b_read1)
    act_low = act_full.astype(bf16)
    grad_full = blocks_to_wide(grad_full)
    grad_pre = (nt(grad_full, w_read2) * slope).astype(bf16)
    grad_b_read1 = jnp.sum(grad_pre.astype(f32), axis=0)
    (grad_out,) = ex(
        "scatter_g", 8, ("rs", nt(grad_pre, w_read1).astype(bf16).reshape(mp_size, share[1], width))
    )
    (readout,) = ex(
        "scatter_readout", 9, ("rs", wide_to_blocks(nn(act_low, w_read2).astype(bf16), mp_size))
    )
    readout = (readout + b_read2).astype(bf16).reshape(images, half, half, -1)
    grad_w_read2 = tn(act_low, grad_full)
    grad_w_read1 = tn(top, grad_pre)

    def to_channels(name, collective, *values):
        stacked = jnp.concatenate([wide_to_blocks(value, mp_size) for value in values], axis=1)
        (result,) = ex(name, collective, ("a2a", stacked))
        parts, start = [], 0
        for value in values:
            part = result[:, start : start + value.shape[0]]
            start += value.shape[0]
            parts.append(part)
        return parts

    def backward(index, grad_scaled, saved):
        norm, conv, act, pooled, pre_down, squeeze, excite, scaled, own_h = saved
        here = sides[index]
        gate_grad = jnp.sum(grad_scaled * act, axis=1)
        grad_up = gate_grad * excite * (1.0 - excite)
        (grad_squeeze,) = ex(
            "squeeze_back", 10 + index, ("psum", exact(grad_up, se_up[index].astype(f32).T))
        )
        grad_down = grad_squeeze * silu_grad(pre_down)
        grad_pooled = exact(grad_down, se_down[index].astype(f32).T)
        grad_act = grad_scaled * excite[:, None, :] + grad_pooled[:, None, :] / (here * here)
        grad_conv = (grad_act * silu_grad(conv)).astype(bf16).reshape(rows[index], -1)
        taps = shifted(grad_conv, images, here)
        grad_w_conv = tn(taps, norm).reshape(9, local, width)
        taps_weight = jnp.swapaxes(w_conv[index], 0, 1).reshape(9 * local, width)
        partial_norm = nn(taps, taps_weight).astype(bf16)
        (grad_norm,) = ex(
            "scatter_norm", 12 + index, ("rs", partial_norm.reshape(mp_size, share[index], width))
        )
        normed, inv_std = normalize(own_h)
        grad_gain = jnp.sum(grad_norm * normed, axis=0)
        grad_shift = jnp.sum(grad_norm, axis=0)
        scaled_grad = grad_norm * gains[index]
        grad_h = (
            inv_std
            * (
                scaled_grad
                - jnp.mean(scaled_grad, axis=1, keepdims=True)
                - normed * jnp.mean(scaled_grad * normed, axis=1, keepdims=True)
            )
        ).astype(bf16)
        small = (
            exact(squeeze.T, grad_up),
            jnp.sum(grad_up, axis=0),
            exact(pooled.T, grad_down),
            jnp.sum(grad_down, axis=0),
        )
        return grad_w_conv, grad_h, jnp.stack([grad_gain, grad_shift]), small

    grad_low = grad_out.astype(bf16)
    gs1, gy1 = to_channels("spread1", 14, nn(grad_low, wide_out[1]).astype(bf16), grad_low)
    gs1 = gs1.astype(f32).reshape(images, half * half, local)
    grad_w_out1 = tn(gy1.reshape(rows[1], local), scaled1)
    grad_w_conv1, grad_h1, lines1, small1 = backward(1, gs1, second)
    grad_value = (grad_out + nn(grad_h1, wide_in[1])) * 0.25
    grad_value_low = grad_value.astype(bf16)
    gs0, gy0, gh1 = to_channels(
        "spread0", 15, nn(grad_value_low, wide_out[0]).astype(bf16), grad_value_low, grad_h1
    )
    grad_w_in1 = tn(gh1.reshape(rows[1], local), value_low)
    grad_w_out0 = 4.0 * tn(gy0.reshape(rows[1], local), mean_scaled)
    residual = spread(gy0.astype(f32).reshape(rows[1], local), images, half)
    gs0 = spread(gs0.astype(f32).reshape(rows[1], local), images, half)
    grad_w_conv0, grad_h0, lines0, small0 = backward(
        0, gs0.reshape(images, side * side, local), first
    )
    grad_in = nn(grad_h0, wide_in[0]).astype(bf16)
    lines = jnp.concatenate([lines0, lines1], axis=0)
    stacked = jnp.concatenate(
        [wide_to_blocks(grad_in, mp_size), wide_to_blocks(grad_h0, mp_size)], axis=1
    )
    spread_all, lines = ex(
        "spread_last", 16, ("a2a", stacked), ("rs", wide_to_blocks(lines, mp_size))
    )
    grad_features = spread_all[:, : share[0]].astype(f32).reshape(rows[0], local) + residual
    grad_features = grad_features.reshape(images, side, side, local)
    grad_w_in0 = tn(spread_all[:, share[0] :].reshape(rows[0], local), feats)

    def parted(value, axis):
        shape = value.shape
        split = value.reshape(shape[:axis] + (dp_size, shape[axis] // dp_size) + shape[axis + 1 :])
        return jnp.moveaxis(split, axis, 0)

    scattered = dp_scatter(
        dp_size,
        [
            parted(jnp.stack([grad_w_in0, grad_w_in1]).astype(bf16), 2),
            parted(jnp.stack([grad_w_conv0, grad_w_conv1]).astype(bf16), 3),
            parted(jnp.stack([small0[2], small1[2]]).astype(bf16), 2),
            parted(jnp.stack([small0[0], small1[0]]).astype(bf16), 1),
            parted(jnp.stack([grad_w_out0, grad_w_out1]).astype(bf16), 2),
            parted(grad_w_read1.astype(bf16), 0),
            parted(grad_w_read2.astype(bf16), 1),
        ],
    )
    vectors = lax.psum(
        (
            lines[0::2],
            lines[1::2],
            jnp.stack([small0[3], small1[3]]),
            jnp.stack([small0[1], small1[1]]),
            grad_b_read1,
            grad_b_read2,
        ),
        "dp",
    )
    return (
        readout,
        grad_features,
        scattered[0],
        vectors[0],
        vectors[1],
        jnp.swapaxes(scattered[1], 1, 2),
        scattered[2],
        vectors[2],
        scattered[3],
        vectors[3],
        scattered[4],
        scattered[5],
        vectors[4],
        scattered[6],
        vectors[5],
    )


def on_device_fast(
    mp_size,
    dp_size,
    features,
    w_in,
    ln_gain,
    ln_bias,
    w_conv,
    se_down,
    se_down_bias,
    se_up,
    se_up_bias,
    w_out,
    w_read1,
    b_read1,
    w_read2,
    b_read2,
    out_grad,
    box_counts,
):
    images, side, _, width = features.shape
    half = side // 2
    local = w_in.shape[1]
    rows = (images * side * side, images * half * half)
    sides = (side, half)
    share = (rows[0] // mp_size, rows[1] // mp_size)
    mp = lax.axis_index("mp")

    def ex(name, collective, *pairs):
        return exchange(name, collective, mp_size, *pairs)

    feats = features.reshape(rows[0], width)
    grad_top = (
        out_grad.astype(f32) * box_counts.astype(f32)[:, None, None, None]
    ).astype(bf16).reshape(rows[1], -1)
    grad_b_read2 = jnp.sum(grad_top.astype(f32), axis=0)
    wc = jnp.swapaxes(w_conv, 1, 2).reshape(2, 9 * local, width)
    (
        norm0,
        norm1,
        conv0,
        conv1,
        gates,
        own_h0,
        own_h1,
        mean_scaled,
        scaled1,
        value_low,
        top,
        act_low,
        grad_pre,
        grad_out,
        weights,
        vectors,
        grad_full,
    ) = run_forward(
        feats,
        w_in,
        w_out,
        wc,
        grad_top,
        w_read1,
        w_read2,
        jnp.concatenate([ln_gain, ln_bias], axis=0),
        (se_down, se_down_bias, se_up, se_up_bias, b_read1.reshape(1, -1)),
        selections(),
    )

    def slim(value):
        return value.reshape(8, 40, value.shape[-1])[:, :36].reshape(288, value.shape[-1])

    weights = weights.reshape(4, width, width)
    wide_in = (weights[0], weights[2])
    wide_out = (weights[1], weights[3])
    vectors = jnp.swapaxes(vectors.reshape(8, 4, local), 0, 1).reshape(4, width)
    gains, shifts = vectors[:2], vectors[2:]
    mean_scaled = slim(blocks_to_wide(mean_scaled.reshape(8, 320, local)))
    scaled1 = slim(blocks_to_wide(scaled1.reshape(8, 320, local)))
    value_low = slim(value_low)
    grad_full = blocks_to_wide(grad_full.reshape(8, 288, -1))
    norm1 = norm1.reshape(2, 12, 16, width)[:, :, :12].reshape(288, width)
    conv1 = conv1.reshape(2, 12, 16, local)[:, :, :12].reshape(2, 144, local)
    conv0 = conv0.reshape(2, 576, local)

    def saved(index, norm, conv, own_h):
        pooled, excite = gates[index, :2, :128], gates[index, :2, 128:256]
        pre_down = gates[index, :2, 256:]
        act = jax.nn.silu(conv)
        return norm, conv, act, pooled, pre_down, jax.nn.silu(pre_down), excite, None, own_h

    first = saved(0, norm0, conv0, own_h0)
    second = saved(1, norm1, conv1, own_h1[:36])
    grad_b_read1 = jnp.sum(grad_pre.astype(f32), axis=0)
    (grad_out,) = ex("scatter_g", 8, ("rs", grad_out[:, :36]))
    (readout,) = ex(
        "scatter_readout", 9, ("rs", wide_to_blocks(nn(act_low, w_read2).astype(bf16), mp_size))
    )
    readout = (readout + b_read2).astype(bf16).reshape(images, half, half, -1)
    grad_w_read2 = tn(act_low, grad_full)
    grad_w_read1 = tn(top, grad_pre)

    def to_channels(name, collective, *values):
        stacked = jnp.concatenate([wide_to_blocks(value, mp_size) for value in values], axis=1)
        (result,) = ex(name, collective, ("a2a", stacked))
        parts, start = [], 0
        for value in values:
            part = result[:, start : start + value.shape[0]]
            start += value.shape[0]
            parts.append(part)
        return parts

    def backward(index, grad_scaled, saved):
        norm, conv, act, pooled, pre_down, squeeze, excite, scaled, own_h = saved
        here = sides[index]
        gate_grad = jnp.sum(grad_scaled * act, axis=1)
        grad_up = gate_grad * excite * (1.0 - excite)
        (grad_squeeze,) = ex(
            "squeeze_back", 10 + index, ("psum", exact(grad_up, se_up[index].astype(f32).T))
        )
        grad_down = grad_squeeze * silu_grad(pre_down)
        grad_pooled = exact(grad_down, se_down[index].astype(f32).T)
        grad_act = grad_scaled * excite[:, None, :] + grad_pooled[:, None, :] / (here * here)
        grad_conv = (grad_act * silu_grad(conv)).astype(bf16).reshape(rows[index], -1)
        taps = shifted(grad_conv, images, here)
        grad_w_conv = tn(taps, norm).reshape(9, local, width)
        taps_weight = jnp.swapaxes(w_conv[index], 0, 1).reshape(9 * local, width)
        partial_norm = nn(taps, taps_weight).astype(bf16)
        (grad_norm,) = ex(
            "scatter_norm", 12 + index, ("rs", partial_norm.reshape(mp_size, share[index], width))
        )
        normed, inv_std = normalize(own_h)
        grad_gain = jnp.sum(grad_norm * normed, axis=0)
        grad_shift = jnp.sum(grad_norm, axis=0)
        scaled_grad = grad_norm * gains[index]
        grad_h = (
            inv_std
            * (
                scaled_grad
                - jnp.mean(scaled_grad, axis=1, keepdims=True)
                - normed * jnp.mean(scaled_grad * normed, axis=1, keepdims=True)
            )
        ).astype(bf16)
        small = (
            exact(squeeze.T, grad_up),
            jnp.sum(grad_up, axis=0),
            exact(pooled.T, grad_down),
            jnp.sum(grad_down, axis=0),
        )
        return grad_w_conv, grad_h, jnp.stack([grad_gain, grad_shift]), small

    grad_low = grad_out.astype(bf16)
    gs1, gy1 = to_channels("spread1", 14, nn(grad_low, wide_out[1]).astype(bf16), grad_low)
    gs1 = gs1.astype(f32).reshape(images, half * half, local)
    grad_w_out1 = tn(gy1.reshape(rows[1], local), scaled1)
    grad_w_conv1, grad_h1, lines1, small1 = backward(1, gs1, second)
    grad_value = (grad_out + nn(grad_h1, wide_in[1])) * 0.25
    grad_value_low = grad_value.astype(bf16)
    gs0, gy0, gh1 = to_channels(
        "spread0", 15, nn(grad_value_low, wide_out[0]).astype(bf16), grad_value_low, grad_h1
    )
    grad_w_in1 = tn(gh1.reshape(rows[1], local), value_low)
    grad_w_out0 = 4.0 * tn(gy0.reshape(rows[1], local), mean_scaled)
    residual = spread(gy0.astype(f32).reshape(rows[1], local), images, half)
    gs0 = spread(gs0.astype(f32).reshape(rows[1], local), images, half)
    grad_w_conv0, grad_h0, lines0, small0 = backward(
        0, gs0.reshape(images, side * side, local), first
    )
    grad_in = nn(grad_h0, wide_in[0]).astype(bf16)
    lines = jnp.concatenate([lines0, lines1], axis=0)
    stacked = jnp.concatenate(
        [wide_to_blocks(grad_in, mp_size), wide_to_blocks(grad_h0, mp_size)], axis=1
    )
    spread_all, lines = ex(
        "spread_last", 16, ("a2a", stacked), ("rs", wide_to_blocks(lines, mp_size))
    )
    grad_features = spread_all[:, : share[0]].astype(f32).reshape(rows[0], local) + residual
    grad_features = grad_features.reshape(images, side, side, local)
    grad_w_in0 = tn(spread_all[:, share[0] :].reshape(rows[0], local), feats)

    def parted(value, axis):
        shape = value.shape
        split = value.reshape(shape[:axis] + (dp_size, shape[axis] // dp_size) + shape[axis + 1 :])
        return jnp.moveaxis(split, axis, 0)

    scattered = dp_scatter(
        dp_size,
        [
            parted(jnp.stack([grad_w_in0, grad_w_in1]).astype(bf16), 2),
            parted(jnp.stack([grad_w_conv0, grad_w_conv1]).astype(bf16), 3),
            parted(jnp.stack([small0[2], small1[2]]).astype(bf16), 2),
            parted(jnp.stack([small0[0], small1[0]]).astype(bf16), 1),
            parted(jnp.stack([grad_w_out0, grad_w_out1]).astype(bf16), 2),
            parted(grad_w_read1.astype(bf16), 0),
            parted(grad_w_read2.astype(bf16), 1),
        ],
    )
    vectors = lax.psum(
        (
            lines[0::2],
            lines[1::2],
            jnp.stack([small0[3], small1[3]]),
            jnp.stack([small0[1], small1[1]]),
            grad_b_read1,
            grad_b_read2,
        ),
        "dp",
    )
    return (
        readout,
        grad_features,
        scattered[0],
        vectors[0],
        vectors[1],
        jnp.swapaxes(scattered[1], 1, 2),
        scattered[2],
        vectors[2],
        scattered[3],
        vectors[3],
        scattered[4],
        scattered[5],
        vectors[4],
        scattered[6],
        vectors[5],
    )


def solution(mesh):
    in_specs = (
        P("dp", None, None, None),
        P(None, "mp", None),
        P(None, "mp"),
        P(None, "mp"),
        P(None, "mp", None, None),
        P(None, "mp", None),
        P(),
        P(None, None, "mp"),
        P(None, "mp"),
        P(None, "mp", None),
        P(None, "mp"),
        P("mp"),
        P("mp", None),
        P("mp"),
        P("dp", None, None, "mp"),
        P("dp"),
    )
    out_specs = (
        P("dp", None, None, "mp"),
        P("dp", None, None, "mp"),
        P(None, "mp", "dp"),
        P(None, "mp"),
        P(None, "mp"),
        P(None, "mp", None, "dp"),
        P(None, "mp", "dp"),
        P(),
        P(None, "dp", "mp"),
        P(None, "mp"),
        P(None, "mp", "dp"),
        P("dp", "mp"),
        P("mp"),
        P("mp", "dp"),
        P("mp"),
    )
    small = mesh.shape["mp"] == 8 and mesh.shape["dp"] == 4
    body = partial(on_device_fast if small else on_device, mesh.shape["mp"], mesh.shape["dp"])
    return jax.shard_map(
        body, mesh=mesh, in_specs=in_specs, out_specs=out_specs, check_vma=False
    )
```

```python
import math
from functools import partial

import jax
import jax.numpy as jnp
import numpy as np
from jax import lax
from jax.experimental import pallas as pl
from jax.experimental.pallas import tpu as pltpu
from jax.sharding import PartitionSpec as P

epsilon = 1e-06
highest = lax.Precision.HIGHEST
f32 = jnp.float32
bf16 = jnp.bfloat16
MESH = pl.DeviceIdType.MESH
VMEM_LIMIT = 56 << 20


def vmem_specs(count):
    return [pl.BlockSpec(memory_space=pltpu.VMEM)] * count


def barrier(peers):
    sem = pltpu.get_barrier_semaphore()
    for peer in peers:
        pl.semaphore_signal(sem, inc=1, device_id=peer, device_id_type=MESH)
    pl.semaphore_wait(sem, len(peers))


def sent(src, dst, send_sem, recv_sem, peer):
    return pltpu.make_async_remote_copy(
        src_ref=src,
        dst_ref=dst,
        send_sem=send_sem,
        recv_sem=recv_sem,
        device_id=peer,
        device_id_type=MESH,
    )


def exchange_kernel(size, kinds, *refs):
    count = len(kinds)
    sources, results = refs[:count], refs[count : 2 * count]
    slots = list(refs[2 * count : -2])
    send_sem, recv_sem = refs[-2:]
    landing = [slots.pop(0) if kind in ("rs", "psum") else result for kind, result in zip(kinds, results)]
    dp, mp = lax.axis_index("dp"), lax.axis_index("mp")
    peers = [(dp, lax.rem(mp + step, size)) for step in range(1, size)]
    barrier(peers)
    copies = []
    for index, kind in enumerate(kinds):
        for step, peer in enumerate(peers):
            src = sources[index].at[peer[1]] if kind in ("rs", "a2a") else sources[index]
            copy = sent(
                src, landing[index].at[mp], send_sem.at[index, step], recv_sem.at[index, step], peer
            )
            copy.start()
            copies.append(copy)
    for index, kind in enumerate(kinds):
        if kind in ("rs", "a2a"):
            landing[index][mp] = sources[index][mp]
        else:
            landing[index][mp] = sources[index][...]
    for copy in copies:
        copy.wait()
    for index, kind in enumerate(kinds):
        if kind in ("rs", "psum"):
            total = landing[index][0].astype(f32)
            for step in range(1, size):
                total = total + landing[index][step].astype(f32)
            results[index][...] = total


def exchange(name, collective, size, *pairs):
    kinds = tuple(kind for kind, value in pairs)
    values = [value for kind, value in pairs]
    shapes, scratch = [], []
    for kind, value in pairs:
        block = value.shape[1:] if kind in ("rs", "a2a") else value.shape
        if kind in ("rs", "psum"):
            shapes.append(jax.ShapeDtypeStruct(block, f32))
            scratch.append(pltpu.VMEM((size,) + block, value.dtype))
        else:
            shapes.append(jax.ShapeDtypeStruct((size,) + block, value.dtype))
    sems = pltpu.SemaphoreType.DMA((len(pairs), size - 1))
    return pl.pallas_call(
        partial(exchange_kernel, size, kinds),
        name=name,
        out_shape=shapes,
        in_specs=vmem_specs(len(values)),
        out_specs=vmem_specs(len(values)),
        scratch_shapes=scratch + [sems, sems],
        compiler_params=pltpu.CompilerParams(
            collective_id=collective, has_side_effects=True, vmem_limit_bytes=VMEM_LIMIT
        ),
    )(*values)


def weights_kernel(size, w_ref, gb_ref, out_ref, gb_out, ss, rs, cs, cr, gs, gr):
    dp, mp = lax.axis_index("dp"), lax.axis_index("mp")
    core = lax.rem(dp, 2)
    sibling = (dp + 1 - 2 * core, mp)
    peers = [(dp, lax.rem(mp + step, size)) for step in range(1, size)]
    barrier(peers + [sibling])
    count, rows = w_ref.shape[0], w_ref.shape[1]
    half = rows // 2
    mine = pl.ds(pl.multiple_of(core * half, half), half)

    def part(owner):
        return pl.ds(pl.multiple_of(owner * rows + core * half, half), half)

    copies = []
    for step, peer in enumerate(peers):
        copy = sent(gb_ref, gb_out.at[mp], gs.at[step], gr.at[step], peer)
        copy.start()
        copies.append(copy)
    outgoing = {}
    for which in range(count):
        for step, peer in enumerate(peers):
            copy = sent(
                w_ref.at[which, mine],
                out_ref.at[which, part(mp)],
                ss.at[which, step],
                rs.at[which, step],
                peer,
            )
            copy.start()
            outgoing[which, step] = copy
    gb_out[mp] = gb_ref[...]
    for which in range(count):
        out_ref[which, pl.ds(pl.multiple_of(mp * rows, rows), rows), :] = w_ref[which]
    for which in range(count):
        for step in range(size - 1):
            owner = lax.rem(mp + size - 1 - step, size)
            outgoing[which, step].wait_recv()
            copy = sent(
                out_ref.at[which, part(owner)],
                out_ref.at[which, part(owner)],
                cs.at[which, step],
                cr.at[which, step],
                sibling,
            )
            copy.start()
            copies.append(copy)
    for copy in outgoing.values():
        copy.wait_send()
    for copy in copies:
        copy.wait()


def gather_weights(size, weights, vectors):
    count, rows, width = weights.shape
    sem = pltpu.SemaphoreType.DMA((count, size - 1))
    vector_sem = pltpu.SemaphoreType.DMA((size - 1,))
    return pl.pallas_call(
        partial(weights_kernel, size),
        name="gather_weights",
        out_shape=[
            jax.ShapeDtypeStruct((count, rows * size, width), weights.dtype),
            jax.ShapeDtypeStruct((size,) + vectors.shape, vectors.dtype),
        ],
        in_specs=vmem_specs(2),
        out_specs=vmem_specs(2),
        scratch_shapes=[sem, sem, sem, sem, vector_sem, vector_sem],
        compiler_params=pltpu.CompilerParams(
            collective_id=1, has_side_effects=True, vmem_limit_bytes=VMEM_LIMIT
        ),
    )(weights, vectors)


def dp_kernel(size, *refs):
    count = (len(refs) - 4) // 4
    sources = refs[:count]
    results = refs[count : 2 * count]
    first = refs[2 * count : 3 * count]
    second = refs[3 * count : 4 * count]
    cs, cr, ys, yr = refs[4 * count :]
    dp, mp = lax.axis_index("dp"), lax.axis_index("mp")
    core = lax.rem(dp, 2)
    y = lax.div(dp, 2)
    chips = size // 2
    sibling = (dp + 1 - 2 * core, mp)
    others = [(2 * lax.rem(y + step, chips) + core, mp) for step in range(1, chips)]
    barrier([sibling] + others)
    copies = []
    for index in range(count):
        for chip in range(chips):
            copy = sent(
                sources[index].at[2 * chip + 1 - core],
                first[index].at[chip],
                cs.at[index, chip],
                cr.at[index, chip],
                sibling,
            )
            copy.start()
            copies.append(copy)
    late = []
    for index in range(count):
        for chip in range(chips):
            copies[index * chips + chip].wait_recv()
            first[index][chip] = (
                first[index][chip].astype(f32) + sources[index][2 * chip + core].astype(f32)
            ).astype(first[index].dtype)
        for step, peer in enumerate(others):
            copy = sent(
                first[index].at[lax.rem(y + step + 1, chips)],
                second[index].at[step],
                ys.at[index, step],
                yr.at[index, step],
                peer,
            )
            copy.start()
            late.append((index, copy))
    for index in range(count):
        total = first[index][y].astype(f32)
        for step in range(chips - 1):
            late[index * (chips - 1) + step][1].wait_recv()
            total = total + second[index][step].astype(f32)
        results[index][...] = total
    for copy in copies:
        copy.wait_send()
    for index, copy in late:
        copy.wait_send()


def dp_scatter(size, values):
    count, chips = len(values), size // 2
    first = [pltpu.VMEM((chips,) + value.shape[1:], value.dtype) for value in values]
    second = [pltpu.VMEM((max(chips - 1, 1),) + value.shape[1:], value.dtype) for value in values]
    core_sem = pltpu.SemaphoreType.DMA((count, chips))
    y_sem = pltpu.SemaphoreType.DMA((count, max(chips - 1, 1)))
    return pl.pallas_call(
        partial(dp_kernel, size),
        name="dp_scatter",
        out_shape=[jax.ShapeDtypeStruct(value.shape[1:], f32) for value in values],
        in_specs=vmem_specs(count),
        out_specs=vmem_specs(count),
        scratch_shapes=first + second + [core_sem, core_sem, y_sem, y_sem],
        compiler_params=pltpu.CompilerParams(
            collective_id=2, has_side_effects=True, vmem_limit_bytes=VMEM_LIMIT
        ),
    )(*values)


def nt(left, right):
    return lax.dot_general(left, right, (((1,), (1,)), ((), ())), preferred_element_type=f32)


def nn(left, right):
    return lax.dot_general(left, right, (((1,), (0,)), ((), ())), preferred_element_type=f32)


def tn(left, right):
    return lax.dot_general(left, right, (((0,), (0,)), ((), ())), preferred_element_type=f32)


def exact(left, right):
    return jnp.dot(left, right, precision=highest)


def blocks_to_wide(value):
    return jnp.swapaxes(value, 0, 1).reshape(value.shape[1], -1)


def wide_to_blocks(value, count):
    return jnp.swapaxes(value.reshape(value.shape[0], count, -1), 0, 1)


def normalize(h):
    mean = jnp.mean(h, axis=1, keepdims=True)
    centered = h - mean
    inv_std = lax.rsqrt(jnp.mean(centered * centered, axis=1, keepdims=True) + epsilon)
    return centered * inv_std, inv_std


def conv_forward(norm, w_conv, images, side):
    width = norm.shape[1]
    out = lax.conv_general_dilated(
        norm.reshape(images, side, side, width),
        w_conv.reshape(w_conv.shape[0], 3, 3, width),
        (1, 1),
        ((1, 1), (1, 1)),
        dimension_numbers=("NHWC", "OHWI", "NHWC"),
        preferred_element_type=f32,
    )
    return out.reshape(images, side * side, -1)


def shifted(grad_conv, images, side):
    width = grad_conv.shape[1]
    padded = jnp.pad(grad_conv.reshape(images, side, side, width), ((0, 0), (1, 1), (1, 1), (0, 0)))
    parts = [
        padded[:, 2 - tap // 3 : 2 - tap // 3 + side, 2 - tap % 3 : 2 - tap % 3 + side, :]
        for tap in range(9)
    ]
    return jnp.stack(parts, axis=3).reshape(images * side * side, 9 * width)


def pool(value, images, side):
    half = side // 2
    shape = (images, half, 2, half, 2, value.shape[-1])
    return jnp.mean(value.astype(f32).reshape(shape), axis=(2, 4)).reshape(images * half * half, -1)


def spread(value, images, half):
    grid = value.reshape(images, half, 1, half, 1, value.shape[-1])
    full = jnp.broadcast_to(grid, (images, half, 2, half, 2, value.shape[-1]))
    return full.reshape(images * 4 * half * half, -1)


def gelu_parts(value):
    cdf = 0.5 * (1.0 + lax.erf(value * (0.5**0.5)))
    pdf = jnp.exp(-0.5 * value * value) * ((2.0 * jnp.pi) ** -0.5)
    return value * cdf, cdf + value * pdf


def silu_grad(value):
    gate = jax.nn.sigmoid(value)
    return gate * (1.0 + value * (1.0 - gate))


def row_share(value, start, rows):
    return lax.dynamic_slice_in_dim(value, start, rows, 0)


def dot(left, right, left_dim, right_dim):
    return lax.dot_general(
        left, right, (((left_dim,), (right_dim,)), ((), ())), preferred_element_type=f32
    )


def exact_dot(left, right, left_dim=1, right_dim=0):
    return lax.dot_general(
        left,
        right,
        (((left_dim,), (right_dim,)), ((), ())),
        precision=highest,
        preferred_element_type=f32,
    )


class Place:
    def __init__(self):
        self.dp, self.mp = lax.axis_index("dp"), lax.axis_index("mp")
        self.z, self.x = lax.div(self.mp, 2), lax.rem(self.mp, 2)
        self.y, self.core = lax.div(self.dp, 2), lax.rem(self.dp, 2)
        self.other_x = 1 - self.x
        self.z_peers = {k: (self.dp, 2 * lax.rem(self.z + k, 4) + self.x) for k in (1, 3, 2)}
        self.z_from = {k: lax.rem(self.z + 4 - k, 4) for k in (0, 1, 3, 2)}
        self.x_peer = (self.dp, 2 * self.z + self.other_x)
        self.y_peer = (2 * (1 - self.y) + self.core, self.mp)
        self.core_peer = (2 * self.y + 1 - self.core, self.mp)
        self.mp_peers = {k: (self.dp, lax.rem(self.mp + k, 8)) for k in range(1, 8)}

    def greet(self, others=()):
        barrier(list(self.mp_peers.values()) + [self.y_peer, self.core_peer] + list(others))


class Flight:
    def __init__(self):
        self.sends = []

    def remote(self, src, dst, send_sem, recv_sem, peer):
        copy = sent(src, dst, send_sem, recv_sem, peer)
        copy.start()
        self.sends.append(copy)
        return copy

    def drain(self):
        for copy in self.sends:
            copy.wait_send()
        self.sends = []


def gather_start(place, flight, buf, zs, zr, xs, xr):
    own = buf.at[place.z, place.x]
    first = {}
    for k, peer in place.z_peers.items():
        first[k] = flight.remote(own, own, zs.at[k], zr.at[k], peer)
    second = {0: flight.remote(own, own, xs.at[0], xr.at[0], place.x_peer)}
    return first, second


def gather_turn(place, flight, buf, xs, xr, first, second):
    for k in (1, 3, 2):
        first[k].wait_recv()
        block = buf.at[place.z_from[k], place.x]
        second[k] = flight.remote(block, block, xs.at[k], xr.at[k], place.x_peer)


def gather_end(second):
    for copy in second.values():
        copy.wait_recv()


def sum_small(place, flight, own, slots, ss, rs):
    copies = []
    for k, peer in place.mp_peers.items():
        copies.append(flight.remote(own, slots.at[k - 1], ss.at[k - 1], rs.at[k - 1], peer))
    total = own[...]
    for k, copy in enumerate(copies):
        copy.wait_recv()
        total = total + slots[k]
    return total


def normalize_rows(h_ref, norm_ref, gain, shift, rows, step):
    @pl.loop(0, rows // step)
    def _(index):
        part = pl.ds(pl.multiple_of(index * step, step), step)
        h = h_ref[part, :]
        mean = jnp.mean(h, axis=1, keepdims=True)
        centered = h - mean
        var = jnp.mean(centered * centered, axis=1, keepdims=True)
        norm_ref[part, :] = (centered * lax.rsqrt(var + epsilon) * gain + shift).astype(bf16)


def conv_grid(norm_ref, start, wc_ref, y_ref, side_ref, side, stride, masks):
    rows = side * stride
    for a in range(3):
        columns = pl.ds(a * 384, 384)
        y_ref[pl.ds(stride, rows), columns] = dot(
            norm_ref[pl.ds(start, rows), :], wc_ref[columns, :], 1, 1
        )
    sums = []
    for b in range(3):
        total = y_ref[pl.ds(0, rows), pl.ds(b * 128, 128)]
        total = total + y_ref[pl.ds(stride, rows), pl.ds(384 + b * 128, 128)]
        total = total + y_ref[pl.ds(2 * stride, rows), pl.ds(768 + b * 128, 128)]
        sums.append(total)
    side_ref[0, pl.ds(8, rows), :] = sums[0]
    side_ref[1, pl.ds(8, rows), :] = sums[2]
    left = side_ref[0, pl.ds(7, rows), :]
    right = side_ref[1, pl.ds(9, rows), :]
    if masks is not None:
        left, right = left * masks[0], right * masks[1]
    return sums[1] + left + right


def column_index(side, stride):
    shape = (side, stride, 128)
    return lax.broadcasted_iota(jnp.int32, shape, 1).reshape(side * stride, 128)


def edge_masks(side):
    column = column_index(side, side)
    return (column > 0).astype(f32), (column < side - 1).astype(f32)


def inner_mask(side, stride):
    return (column_index(side, stride) < side).astype(f32)


def forward_kernel(
    feats,
    w_in,
    w_out,
    wc,
    dout,
    w_read1,
    w_read2,
    lines,
    se_down,
    se_down_bias,
    se_up,
    se_up_bias,
    b_read1,
    pool_mat,
    wide_mat,
    slim_mat,
    pack_mat,
    unpack_mat,
    o_norm0,
    o_norm1,
    o_conv0,
    o_conv1,
    o_se,
    o_h0,
    o_h1,
    o_mean,
    o_scaled,
    o_value,
    o_top,
    o_act,
    o_dpre,
    o_g,
    o_w,
    o_lines,
    o_dout,
    o_ro,
    v_feats,
    v_w,
    v_wc,
    v_read1,
    v_read2,
    v_dout,
    v_h,
    v_norm0,
    v_y,
    v_side,
    v_y1,
    v_side1,
    v_lines,
    v_conv0,
    v_act0,
    v_mean,
    v_wide,
    v_value,
    v_low,
    v_norm1,
    v_norm1e,
    v_conv1,
    v_scaled,
    v_top,
    v_act,
    v_slope,
    v_dpre,
    v_g,
    v_slots,
    v_small,
    v_se,
    v_ro,
    load_sem,
    store_sem,
    wzs,
    wzr,
    wxs,
    wxr,
    wys,
    wyr,
    wcs,
    wcr,
    gzs,
    gzr,
    gxs,
    gxr,
    sms,
    smr,
):
    place = Place()
    flight = Flight()
    z, x, dp, mp = place.z, place.x, place.dp, place.mp
    quarter = w_in.shape[1] // 4
    own_rows = pl.ds(pl.multiple_of(dp * quarter, quarter), quarter)
    weights = (w_in.at[0], w_out.at[0], w_in.at[1], w_out.at[1])

    local = []

    def load(src, dst):
        copy = pltpu.make_async_copy(src, dst, load_sem.at[len(local)])
        copy.start()
        local.append(copy)
        return copy

    stores = []

    def store(src, dst):
        copy = pltpu.make_async_copy(src, dst, store_sem.at[len(stores)])
        copy.start()
        stores.append(copy)

    own_weights = [
        load(weights[which].at[own_rows], v_w.at[which, z, x, dp]) for which in range(4)
    ]
    own_dout = load(dout, v_dout.at[z, x])
    v_lines[z, x] = lines[...]
    got_feats = load(feats, v_feats)
    got_wc0 = load(wc.at[0], v_wc.at[0])
    got_read1 = load(w_read1, v_read1)
    got_read2 = load(w_read2, v_read2)
    got_wc1 = load(wc.at[1], v_wc.at[1])
    place.greet()

    line_flight = gather_start(place, flight, v_lines, gzs.at[0], gzr.at[0], gxs.at[0], gxr.at[0])
    own_weights[0].wait()

    def block(which, k, other, q):
        column = place.other_x if other else x
        return v_w.at[which, place.z_from[k], column, q]

    near, far = dp, 2 * (1 - place.y) + place.core
    first, second, third, fourth = {}, {}, {}, []

    def pass_core(k, other, q, slot):
        src = block(0, k, other, q)
        fourth.append(
            flight.remote(
                src, src, wcs.at[0, k, other, slot], wcr.at[0, k, other, slot], place.core_peer
            )
        )

    def pass_y(k, other):
        src = block(0, k, other, near)
        third[k, other] = flight.remote(
            src, src, wys.at[0, k, other], wyr.at[0, k, other], place.y_peer
        )
        pass_core(k, other, near, 0)

    def pass_x(k):
        src = block(0, k, 0, near)
        second[k] = flight.remote(src, src, wxs.at[0, k], wxr.at[0, k], place.x_peer)

    own = block(0, 0, 0, near)
    for k, peer in place.z_peers.items():
        first[k] = flight.remote(own, own, wzs.at[0, k], wzr.at[0, k], peer)
    pass_x(0)
    pass_y(0, 0)
    for k in (1, 3, 2):
        first[k].wait_recv()
        pass_x(k)
        pass_y(k, 0)
    bulk_z = {}
    for which in (1, 2, 3):
        own_weights[which].wait()
        own = v_w.at[which, z, x, dp]
        for k, peer in place.z_peers.items():
            bulk_z[which, k] = flight.remote(own, own, wzs.at[which, k], wzr.at[which, k], peer)
    for k in (0, 1, 3, 2):
        second[k].wait_recv()
        pass_y(k, 1)
    for other in (0, 1):
        for k in (0, 1, 3, 2):
            third[k, other].wait_recv()
            pass_core(k, other, far, 1)
    gather_turn(place, flight, v_lines, gxs.at[0], gxr.at[0], *line_flight)
    own_dout.wait()
    dout_flight = gather_start(place, flight, v_dout, gzs.at[1], gzr.at[1], gxs.at[1], gxr.at[1])

    images = 2
    grid0, grid1, conv1_rows = v_feats.shape[0] // images, v_low.shape[0] // images, v_norm1e.shape[0] // images
    side0 = 24
    got_feats.wait()
    for image in range(images):
        v_value[pl.ds(image * grid1, grid1), :] = dot(
            pool_mat[...], v_feats[pl.ds(image * grid0, grid0), :], 1, 0
        )
    v_y[...] = jnp.zeros_like(v_y)
    v_y1[...] = jnp.zeros_like(v_y1)
    v_side[...] = jnp.zeros_like(v_side)
    v_side1[...] = jnp.zeros_like(v_side1)
    gather_end(line_flight[1])
    line = jnp.concatenate([v_lines[a, b] for a in range(4) for b in range(2)], axis=1)
    store(v_lines, o_lines)

    for copy in fourth:
        copy.wait_recv()

    def wide_weight(which, index):
        return v_w[which, index].reshape(2 * 4 * quarter, v_w.shape[-1])

    def bulk_x():
        copies = []
        for which in (1, 2, 3):
            for k in (1, 3, 2):
                bulk_z[which, k].wait_recv()
            src = v_w.at[which, :, x, near]
            copies.append(
                flight.remote(src, src, wxs.at[which, 0], wxr.at[which, 0], place.x_peer)
            )
        return copies

    def bulk_y(copies):
        result = []
        for which, copy in zip((1, 2, 3), copies):
            copy.wait_recv()
            src = v_w.at[which, :, :, near]
            result.append(
                flight.remote(src, src, wys.at[which, 0, 0], wyr.at[which, 0, 0], place.y_peer)
            )
        return result

    def bulk_core(copies):
        result = []
        for which, copy in zip((1, 2, 3), copies):
            copy.wait_recv()
            for slot, q in enumerate((near, far)):
                src = v_w.at[which, :, :, q]
                result.append(
                    flight.remote(
                        src,
                        src,
                        wcs.at[which, 0, 0, slot],
                        wcr.at[which, 0, 0, slot],
                        place.core_peer,
                    )
                )
        return result

    bulk = bulk_x()

    @pl.loop(0, 4)
    def _(index):
        columns = pl.ds(pl.multiple_of(index * 256, 256), 256)
        v_h[:, columns] = dot(v_feats[...], wide_weight(0, index), 1, 1)

    share0 = v_h.shape[0] // 8
    store(v_h.at[pl.ds(pl.multiple_of(mp * share0, share0), share0)], o_h0)
    bulk = bulk_y(bulk)
    normalize_rows(v_h, v_norm0, line[0:1], line[2:3], v_h.shape[0], 32)
    store(v_norm0, o_norm0)
    got_wc0.wait()
    masks = edge_masks(side0)
    pooled = []
    for image in range(images):
        conv = conv_grid(
            v_norm0, image * grid0, v_wc.at[0], v_y, v_side, side0, side0, masks
        )
        v_conv0[pl.ds(image * grid0, grid0), :] = conv
        act = conv * jax.nn.sigmoid(conv)
        v_act0[pl.ds(image * grid0, grid0), :] = act
        pooled.append(jnp.sum(act, axis=0, keepdims=True) * (1.0 / grid0))
    store(v_conv0, o_conv0)
    gather_turn(place, flight, v_dout, gxs.at[1], gxr.at[1], *dout_flight)

    def excite(index, pooled):
        pooled = jnp.concatenate(pooled + [jnp.zeros((6, 128), f32)], axis=0)
        v_small[index] = exact_dot(pooled, se_down[index].astype(f32))
        pre = sum_small(
            place, flight, v_small.at[index], v_slots.at[index], sms.at[index], smr.at[index]
        )
        pre = pre + se_down_bias[index : index + 1, :]
        squeeze = pre * jax.nn.sigmoid(pre)
        gate = jax.nn.sigmoid(
            exact_dot(squeeze, se_up[index].astype(f32)) + se_up_bias[index : index + 1, :]
        )
        v_se[index, :, 0:128] = pooled
        v_se[index, :, 128:256] = gate
        v_se[index, :, 256:512] = pre
        return gate

    gate = excite(0, pooled)
    for image in range(images):
        scaled = (v_act0[pl.ds(image * grid0, grid0), :] * gate[image : image + 1, :]).astype(bf16)
        v_mean[z, x, pl.ds(image * grid1, grid1), :] = dot(pool_mat[...], scaled, 1, 0).astype(bf16)
    flying = gather_start(place, flight, v_mean, gzs.at[2], gzr.at[2], gxs.at[2], gxr.at[2])
    gather_turn(place, flight, v_mean, gxs.at[2], gxr.at[2], *flying)
    bulk = bulk_core(bulk)
    gather_end(flying[1])
    store(v_mean, o_mean)
    for copy in bulk:
        copy.wait_recv()
    store(v_w, o_w)

    def widen(src):
        for a in range(4):
            for b in range(2):
                v_wide[:, pl.ds((2 * a + b) * 128, 128)] = src[a, b]

    widen(v_mean)
    for index in range(4):
        columns = pl.ds(index * 256, 256)
        value = v_value[:, columns] + dot(v_wide[...], wide_weight(1, index), 1, 1)
        v_value[:, columns] = value
        v_low[:, columns] = value.astype(bf16)
    store(v_low, o_value)
    rows1 = v_low.shape[0]
    share1 = rows1 // 8
    h1 = v_h.at[pl.ds(0, rows1)]
    stores[1].wait()
    for index in range(4):
        h1[:, pl.ds(index * 256, 256)] = dot(v_low[...], wide_weight(2, index), 1, 1)
    store(h1.at[pl.ds(pl.multiple_of(mp * share1, share1), share1)], o_h1)
    normalize_rows(h1, v_norm1, line[1:2], line[3:4], rows1, 32)
    for image in range(images):
        v_norm1e[pl.ds(image * conv1_rows, conv1_rows), :] = dot(
            wide_mat[...], v_norm1[pl.ds(image * grid1, grid1), :], 1, 0
        ).astype(bf16)
    store(v_norm1e, o_norm1)
    got_wc1.wait()
    inner = inner_mask(12, 16)
    acts, pooled = [], []
    for image in range(images):
        conv = conv_grid(
            v_norm1e, image * conv1_rows, v_wc.at[1], v_y1, v_side1, 12, 16, None
        )
        v_conv1[pl.ds(image * conv1_rows, conv1_rows), :] = conv
        act = conv * jax.nn.sigmoid(conv) * inner
        acts.append(act)
        pooled.append(jnp.sum(act, axis=0, keepdims=True) * (1.0 / 144))
    store(v_conv1, o_conv1)
    gate = excite(1, pooled)
    store(v_se, o_se)
    for image in range(images):
        scaled = (acts[image] * gate[image : image + 1, :]).astype(bf16)
        v_scaled[z, x, pl.ds(image * grid1, grid1), :] = dot(slim_mat[...], scaled, 1, 0).astype(bf16)
    flying = gather_start(place, flight, v_scaled, gzs.at[3], gzr.at[3], gxs.at[3], gxr.at[3])
    gather_turn(place, flight, v_scaled, gxs.at[3], gxr.at[3], *flying)
    gather_end(flying[1])
    store(v_scaled, o_scaled)
    widen(v_scaled)
    slim_rows = v_top.shape[0] // images
    for index in range(4):
        columns = pl.ds(index * 256, 256)
        value = v_value[:, columns] + dot(v_wide[...], wide_weight(3, index), 1, 1)
        value = value.astype(bf16)
        for image in range(images):
            v_top[pl.ds(image * slim_rows, slim_rows), columns] = dot(
                pack_mat[...], value[image * grid1 : (image + 1) * grid1, :], 1, 0
            ).astype(bf16)
    store(v_top, o_top)

    got_read1.wait()
    for index in range(v_act.shape[1] // 256):
        columns = pl.ds(index * 256, 256)
        pre = dot(v_top[...], v_read1[:, columns], 1, 0) + b_read1[:, columns]
        cdf = 0.5 * (1.0 + lax.erf(pre * (0.5**0.5)))
        v_act[:, columns] = (pre * cdf).astype(bf16)
        v_slope[:, columns] = cdf + pre * (jnp.exp(-0.5 * pre * pre) * (2.0 * math.pi) ** -0.5)
    store(v_act, o_act)
    got_read2.wait()
    for owner in range(8):
        v_ro[owner] = dot(v_act[...], v_read2[:, pl.ds(owner * 512, 512)], 1, 0).astype(bf16)
    store(v_ro, o_ro)
    gather_end(dout_flight[1])
    store(v_dout, o_dout)
    width = v_dout.shape[-1]
    for part in range(2):
        hidden = pl.ds(part * 256, 256)
        total = jnp.zeros((v_top.shape[0], 256), f32)
        for a in range(4):
            for b in range(2):
                total = total + dot(
                    v_dout[a, b], v_read2[hidden, pl.ds((2 * a + b) * width, width)], 1, 1
                )
        v_dpre[:, hidden] = (total * v_slope[:, hidden]).astype(bf16)
    store(v_dpre, o_dpre)
    wide_dpre = jnp.concatenate(
        [
            dot(unpack_mat[...], v_dpre[pl.ds(image * slim_rows, slim_rows), :], 1, 0).astype(bf16)
            for image in range(images)
        ],
        axis=0,
    )
    for index in range(4):
        columns = pl.ds(index * 256, 256)
        part = dot(wide_dpre, v_read1[columns, :], 1, 1)
        for owner in range(8):
            v_g[owner, :, columns] = part[owner * share1 : (owner + 1) * share1, :].astype(bf16)
    store(v_g, o_g)
    flight.drain()
    for index, copy in enumerate(stores):
        if index != 1:
            copy.wait()


def selections():
    pool_mat = np.zeros((160, 576), np.float32)
    wide_mat = np.zeros((192, 160), np.float32)
    pack_mat = np.zeros((144, 160), np.float32)
    for row in range(12):
        for column in range(12):
            padded = 40 * (row // 3) + 12 * (row % 3) + column
            wide_mat[16 * row + column, padded] = 1.0
            pack_mat[12 * row + column, padded] = 1.0
            for down in range(2):
                for right in range(2):
                    pool_mat[padded, 24 * (2 * row + down) + 2 * column + right] = 0.25
    return [
        jnp.asarray(mat, bf16) for mat in (pool_mat, wide_mat, wide_mat.T, pack_mat, pack_mat.T)
    ]


def run_forward(feats, w_in, w_out, wc, dout, w_read1, w_read2, lines, smalls, mats):
    def shaped(dtype, *dims):
        return jax.ShapeDtypeStruct(dims, dtype)

    outs = [
        shaped(bf16, 1152, 1024),
        shaped(bf16, 384, 1024),
        shaped(f32, 1152, 128),
        shaped(f32, 384, 128),
        shaped(f32, 2, 8, 512),
        shaped(f32, 144, 1024),
        shaped(f32, 40, 1024),
        shaped(bf16, 4, 2, 320, 128),
        shaped(bf16, 4, 2, 320, 128),
        shaped(bf16, 320, 1024),
        shaped(bf16, 288, 1024),
        shaped(bf16, 288, 512),
        shaped(bf16, 288, 512),
        shaped(bf16, 8, 40, 1024),
        shaped(bf16, 4, 4, 2, 4, 32, 1024),
        shaped(f32, 4, 2, 4, 128),
        shaped(bf16, 4, 2, 288, 512),
        shaped(bf16, 8, 288, 512),
    ]
    scratch = [
        (bf16, 1152, 1024),
        (bf16, 4, 4, 2, 4, 32, 1024),
        (bf16, 2, 1152, 1024),
        (bf16, 1024, 512),
        (bf16, 512, 4096),
        (bf16, 4, 2, 288, 512),
        (f32, 1152, 1024),
        (bf16, 1152, 1024),
        (f32, 624, 1152),
        (f32, 2, 592, 128),
        (f32, 224, 1152),
        (f32, 2, 208, 128),
        (f32, 4, 2, 4, 128),
        (f32, 1152, 128),
        (f32, 1152, 128),
        (bf16, 4, 2, 320, 128),
        (bf16, 320, 1024),
        (f32, 320, 1024),
        (bf16, 320, 1024),
        (bf16, 320, 1024),
        (bf16, 384, 1024),
        (f32, 384, 128),
        (bf16, 4, 2, 320, 128),
        (bf16, 288, 1024),
        (bf16, 288, 512),
        (f32, 288, 512),
        (bf16, 288, 512),
        (bf16, 8, 40, 1024),
        (f32, 2, 7, 8, 256),
        (f32, 2, 8, 256),
        (f32, 2, 8, 512),
        (bf16, 8, 288, 512),
    ]
    dma = pltpu.SemaphoreType.DMA
    sems = [(12,), (20,), (4, 4), (4, 4), (4, 4), (4, 4), (4, 4, 2), (4, 4, 2)]
    sems += [(4, 4, 2, 2), (4, 4, 2, 2), (4, 4), (4, 4), (4, 4), (4, 4), (2, 7), (2, 7)]
    anywhere = [pl.BlockSpec(memory_space=pl.ANY)]
    operands = [feats, w_in, w_out, wc, dout, w_read1, w_read2]
    return pl.pallas_call(
        forward_kernel,
        name="forward",
        out_shape=outs,
        in_specs=anywhere * len(operands) + vmem_specs(1 + len(smalls) + len(mats)),
        out_specs=anywhere * len(outs),
        scratch_shapes=[pltpu.VMEM(dims, dtype) for dtype, *dims in scratch]
        + [dma(shape) for shape in sems],
        compiler_params=pltpu.CompilerParams(
            collective_id=20, has_side_effects=True, vmem_limit_bytes=60 << 20
        ),
    )(*operands, lines, *smalls, *mats)


def sum_start(place, flight, own, slots, ss, rs):
    return [
        flight.remote(own, slots.at[k - 1], ss.at[k - 1], rs.at[k - 1], peer)
        for k, peer in place.mp_peers.items()
    ]


def sum_end(own, slots, copies):
    total = own[...]
    for k, copy in enumerate(copies):
        copy.wait_recv()
        total = total + slots[k]
    return total


def swap_start(place, flight, src, dst, ss, rs):
    copies = [
        flight.remote(src.at[peer[1]], dst.at[place.mp], ss.at[k - 1], rs.at[k - 1], peer)
        for k, peer in place.mp_peers.items()
    ]
    dst[place.mp] = src[place.mp]
    return copies


def received(copies):
    for copy in copies:
        copy.wait_recv()


class Reduce:
    order = (2, 1, 3, 0)

    def __init__(self, place, flight, part, xbuf, zbuf, xs, xr, zs, zr):
        self.place, self.flight = place, flight
        self.part, self.xbuf, self.zbuf = part, xbuf, zbuf
        self.xs, self.xr, self.zs, self.zr = xs, xr, zs, zr
        self.across, self.along = {}, {}

    def target(self, k):
        return lax.rem(self.place.z + k, 4)

    def send_x(self, k):
        self.across[k] = self.flight.remote(
            self.part.at[self.target(k), self.place.other_x],
            self.xbuf.at[k],
            self.xs.at[k],
            self.xr.at[k],
            self.place.x_peer,
        )

    def start(self):
        for k in self.order:
            self.send_x(k)

    def turn(self):
        for k in self.order[:3]:
            self.across[k].wait_recv()
            mine = self.part.at[self.target(k), self.place.x]
            mine[...] = (mine[...].astype(f32) + self.xbuf[k].astype(f32)).astype(bf16)
            self.along[k] = self.flight.remote(
                mine, self.zbuf.at[k - 1], self.zs.at[k], self.zr.at[k], self.place.z_peers[k]
            )

    def finish(self):
        self.across[0].wait_recv()
        for k in (1, 3, 2):
            self.along[k].wait_recv()

    def total(self, rows):
        value = self.part[self.place.z, self.place.x, rows, :].astype(f32)
        value = value + self.xbuf[0, rows, :].astype(f32)
        for k in range(3):
            value = value + self.zbuf[k, rows, :].astype(f32)
        return value


class Unit:
    def __init__(self, place, flight, part, first, last, cs, cr, ys, yr):
        self.place, self.flight = place, flight
        self.part, self.first, self.last = part, first, last
        self.cs, self.cr, self.ys, self.yr = cs, cr, ys, yr

    def start(self):
        place = self.place
        self.near = [
            self.flight.remote(
                self.part.at[2 * chip + 1 - place.core],
                self.first.at[chip],
                self.cs.at[chip],
                self.cr.at[chip],
                place.core_peer,
            )
            for chip in range(2)
        ]

    def turn(self):
        place = self.place
        received(self.near)
        far = 1 - place.y
        mine = self.first.at[far]
        mine[...] = (
            mine[...].astype(f32) + self.part[2 * far + place.core].astype(f32)
        ).astype(mine.dtype)
        self.copy = self.flight.remote(mine, self.last, self.ys, self.yr, place.y_peer)

    def total(self, rows):
        place = self.place
        value = self.first[place.y, rows].astype(f32)
        value = value + self.part[2 * place.y + place.core, rows].astype(f32)
        return value + self.last[rows].astype(f32)


class Stage:
    def __init__(self, buf, sems):
        self.buf, self.sems, self.flying, self.next = buf, sems, {}, 0

    def out(self, value, dst):
        slot = self.next
        self.next = (slot + 1) % self.buf.shape[0]
        if slot in self.flying:
            self.flying[slot].wait()
        self.buf[slot, pl.ds(0, value.shape[0])] = value
        copy = pltpu.make_async_copy(
            self.buf.at[slot, pl.ds(0, value.shape[0])], dst, self.sems.at[slot]
        )
        copy.start()
        self.flying[slot] = copy

    def drain(self):
        for copy in self.flying.values():
            copy.wait()


def silu_slope(value, gate):
    return gate * (1.0 + value * (1.0 - gate))


def taps_of(grad, z_ref, g_ref, start, side, stride, masks):
    rows = side * stride
    z_ref[pl.ds(32, rows), :] = grad
    for a in range(3):
        for b in range(3):
            value = z_ref[pl.ds(32 - stride * (a - 1) - (b - 1), rows), :]
            if masks is not None and b != 1:
                value = value * (masks[1] if b == 0 else masks[0])
            g_ref[pl.ds(start, rows), pl.ds((3 * a + b) * 128, 128)] = value.astype(bf16)


def norm_backward(h_ref, grad_of, gain, acc_ref, out_ref, rows, step):
    acc_ref[...] = jnp.zeros_like(acc_ref)
    for start in range(0, rows, step):
        part = pl.ds(start, step)
        h = h_ref[part, :]
        grad = grad_of(part)
        centered = h - jnp.mean(h, axis=1, keepdims=True)
        inv_std = lax.rsqrt(jnp.mean(centered * centered, axis=1, keepdims=True) + epsilon)
        normed = centered * inv_std
        groups = (step // 8, 8, h.shape[1])
        acc_ref[0] += jnp.sum((grad * normed).reshape(groups), axis=0)
        acc_ref[1] += jnp.sum(grad.reshape(groups), axis=0)
        scaled = grad * gain
        first = jnp.mean(scaled, axis=1, keepdims=True)
        second = jnp.mean(scaled * normed, axis=1, keepdims=True)
        out_ref[part, :] = (inv_std * (scaled - first - normed * second)).astype(bf16)


def backward_kernel(
    g_in,
    ro_in,
    act_in,
    dpre_in,
    top_in,
    dout_in,
    w_in,
    norm0_in,
    norm1_in,
    conv0_in,
    conv1_in,
    h0_in,
    h1_in,
    mean_in,
    scaled_in,
    value_in,
    feats_in,
    wc_in,
    gates,
    lines,
    se_down,
    se_up,
    b_read2,
    wide_mat,
    slim_mat,
    spread_mat,
    o_readout,
    o_features,
    o_read2,
    o_read1,
    o_conv,
    o_io,
    o_se,
    o_vec,
    v_pg,
    v_xg,
    v_zg,
    v_ro,
    v_xro,
    v_zro,
    v_p1,
    v_x1,
    v_z1,
    v_p0,
    v_x0,
    v_z0,
    v_act,
    v_dpre,
    v_top,
    v_dout,
    v_w,
    v_wc,
    v_norm0,
    v_norm1,
    v_conv0,
    v_conv1,
    v_h0,
    v_h1,
    v_mean,
    v_scaled,
    v_value,
    v_feats,
    v_g,
    v_a1s,
    v_a1r,
    v_a2s,
    v_a2r,
    v_a3s,
    v_a3r,
    v_lines_s,
    v_lines_r,
    v_small,
    v_slots,
    v_gs,
    v_zz0,
    v_zz1,
    v_taps0,
    v_taps1,
    v_slim,
    v_acc,
    v_gh,
    v_vec,
    v_vec_r,
    p_read2,
    f_read2,
    y_read2,
    p_read1,
    f_read1,
    y_read1,
    p_conv1,
    f_conv1,
    y_conv1,
    p_conv0,
    f_conv0,
    y_conv0,
    p_io,
    f_io,
    y_io,
    p_in0,
    f_in0,
    y_in0,
    p_se,
    f_se,
    y_se,
    st_wide,
    st_half,
    st_slim,
    st_se,
    load_sem,
    store_sem,
    stage_sem,
    xs,
    xr,
    zs,
    zr,
    as_,
    ar,
    sms,
    smr,
    cs,
    cr,
    ys,
    yr,
    vs,
    vr,
):
    place = Place()
    flight = Flight()
    z, x, dp, mp = place.z, place.x, place.dp, place.mp
    images, local = 2, 128
    width = v_feats.shape[1]
    rows0, rows1 = v_feats.shape[0], v_value.shape[0]
    grid0, grid1, wide1 = rows0 // images, rows1 // images, v_norm1.shape[0] // images
    share0, share1 = rows0 // 8, rows1 // 8
    loads = []

    def load(src, dst):
        copy = pltpu.make_async_copy(src, dst, load_sem.at[len(loads)])
        copy.start()
        loads.append(copy)
        return copy

    def wide_load(src, dst):
        return [
            load(src.at[a, b], dst.at[:, pl.ds((2 * a + b) * local, local)])
            for a in range(4)
            for b in range(2)
        ]

    got_g = load(g_in, v_pg)
    got_act = load(act_in, v_act)
    got_dout = load(dout_in, v_dout)
    got_w3 = load(w_in.at[3], v_w.at[0])
    got_ro = load(ro_in, v_ro)
    got_top = load(top_in, v_top)
    got_dpre = load(dpre_in, v_dpre)
    got_conv1 = load(conv1_in, v_conv1)
    got_scaled = wide_load(scaled_in, v_scaled)
    got_wc1 = load(wc_in.at[1], v_wc)
    got_norm1 = load(norm1_in, v_norm1)
    got_h1 = load(h1_in, v_h1)
    got_w2 = load(w_in.at[2], v_w.at[1])
    got_conv0 = load(conv0_in, v_conv0)
    got_value = load(value_in, v_value)
    got_mean = wide_load(mean_in, v_mean)
    got_norm0 = load(norm0_in, v_norm0)
    got_h0 = load(h0_in, v_h0)
    got_feats = load(feats_in, v_feats)

    place.greet([(lax.rem(dp + 3 - 2 * place.core, 4), mp)])

    def reduce(index, part, xbuf, zbuf):
        return Reduce(
            place, flight, part, xbuf, zbuf, xs.at[index], xr.at[index], zs.at[index], zr.at[index]
        )

    def unit(index, part, first, last):
        return Unit(
            place, flight, part, first, last, cs.at[index], cr.at[index], ys.at[index], yr.at[index]
        )

    reduce_g = reduce(0, v_pg, v_xg, v_zg)
    reduce_ro = reduce(1, v_ro, v_xro, v_zro)
    reduce_1 = reduce(2, v_p1, v_x1, v_z1)
    reduce_0 = reduce(3, v_p0, v_x0, v_z0)
    unit_read2 = unit(0, p_read2, f_read2, y_read2)
    unit_read1 = unit(1, p_read1, f_read1, y_read1)
    unit_conv1 = unit(2, p_conv1, f_conv1, y_conv1)
    unit_conv0 = unit(3, p_conv0, f_conv0, y_conv0)
    unit_io = unit(4, p_io, f_io, y_io)
    unit_in0 = unit(5, p_in0, f_in0, y_in0)
    unit_se = unit(6, p_se, f_se, y_se)
    stage_wide = Stage(st_wide, stage_sem.at[0])
    stage_half = Stage(st_half, stage_sem.at[1])
    stage_slim = Stage(st_slim, stage_sem.at[2])
    stage_se = Stage(st_se, stage_sem.at[3])

    got_g.wait()
    reduce_g.start()
    v_zz0[...] = jnp.zeros_like(v_zz0)
    v_zz1[...] = jnp.zeros_like(v_zz1)
    line = jnp.concatenate([lines[a, b] for a in range(4) for b in range(2)], axis=1)
    got_act.wait()
    got_dout.wait()

    def read2_part(d):
        for b in range(2):
            p_read2[d, :, pl.ds(b * 512, 512)] = dot(v_act[...], v_dout[d, b], 0, 0).astype(bf16)

    read2_part(0)
    reduce_g.turn()
    for d in range(1, 4):
        read2_part(d)
    unit_read2.start()
    reduce_g.finish()
    v_g[...] = reduce_g.total(pl.ds(0, share1))
    got_w3.wait()
    low = v_g[...].astype(bf16)
    for index in range(4):
        columns = pl.ds(index * 256, 256)
        back = dot(low, v_w[0, :, columns], 1, 0)
        own = v_g[:, columns]
        for b in range(2):
            v_a1s[2 * index + b, 0] = back[:, b * local : (b + 1) * local].astype(bf16)
            v_a1s[2 * index + b, 1] = own[:, b * local : (b + 1) * local].astype(bf16)
    swap_1 = swap_start(place, flight, v_a1s, v_a1r, as_.at[0], ar.at[0])
    got_ro.wait()
    reduce_ro.start()
    got_w1 = load(w_in.at[1], v_w.at[0])
    got_top.wait()
    got_dpre.wait()
    for d in range(4):
        p_read1[d] = dot(v_top[:, pl.ds(d * 256, 256)], v_dpre[...], 0, 0).astype(bf16)
    unit_read1.start()
    ones = jnp.ones((8, v_dpre.shape[0]), bf16)
    v_vec[...] = jnp.zeros_like(v_vec)
    v_vec[0:1, :] = dot(ones, v_dpre[...], 1, 0)[0:1]
    v_vec[1:2, :] = dot(ones, v_dout[z, x], 1, 0)[0:1]
    received(swap_1)

    def gathered(buf, which):
        return jnp.concatenate([buf[s, which].astype(f32) for s in range(8)], axis=0).astype(bf16)

    def gate_back(index, sums, overlap):
        pooled, gate = gates[index, :, 0:128], gates[index, :, 128:256]
        pre = gates[index, :, 256:512]
        grad_up = jnp.concatenate(sums + [jnp.zeros((6, local), f32)], axis=0) * gate * (1.0 - gate)
        up_weight = se_up[index].astype(f32)
        v_small[index] = exact_dot(grad_up, up_weight, 1, 1)
        copies = sum_start(
            place, flight, v_small.at[index], v_slots.at[index], sms.at[index], smr.at[index]
        )
        overlap()
        squeeze_gate = jax.nn.sigmoid(pre)
        squeeze = pre * squeeze_gate
        up_grad = exact_dot(squeeze, grad_up, 0, 0)
        grad_down = sum_end(v_small.at[index], v_slots.at[index], copies) * silu_slope(
            pre, squeeze_gate
        )
        down_grad = exact_dot(grad_down, pooled, 0, 0)
        for d in range(4):
            p_se[d, 2 * index] = down_grad[64 * d : 64 * d + 64]
            p_se[d, 2 * index + 1] = up_grad[64 * d : 64 * d + 64]
        v_vec[2:3, index * 256 : index * 256 + 256] = jnp.sum(grad_down, axis=0, keepdims=True)
        v_vec[3:4, index * 128 : index * 128 + 128] = jnp.sum(grad_up, axis=0, keepdims=True)
        return gate, exact_dot(grad_down, se_down[index].astype(f32), 1, 1)

    gs1 = gathered(v_a1r, 0)
    got_conv1.wait()
    inner = inner_mask(12, 16)
    sums = []
    for image in range(images):
        grad = dot(wide_mat[...], gs1[image * grid1 : (image + 1) * grid1], 1, 0)
        v_gs[pl.ds(image * wide1, wide1), :] = grad
        conv = v_conv1[pl.ds(image * wide1, wide1), :]
        sums.append(jnp.sum(grad * conv * jax.nn.sigmoid(conv) * inner, axis=0, keepdims=True))

    def fill_out1():
        received_all(got_scaled)
        gy1 = gathered(v_a1r, 1)
        for d in range(4):
            p_io[d, 0:128, :] = dot(gy1, v_scaled[:, pl.ds(d * 256, 256)], 0, 0).astype(bf16)

    gate, grad_pooled = gate_back(1, sums, fill_out1)
    got_norm1.wait()
    for image in range(images):
        rows = pl.ds(image * wide1, wide1)
        conv = v_conv1[rows, :]
        grad = v_gs[rows, :] * gate[image : image + 1] + grad_pooled[image : image + 1] * (1.0 / 144)
        grad = grad * silu_slope(conv, jax.nn.sigmoid(conv)) * inner
        taps_of(grad, v_zz1, v_taps1, image * wide1, 12, 16, None)
        v_slim[pl.ds(image * grid1, grid1), :] = dot(
            slim_mat[...], v_taps1[rows, :], 1, 0
        ).astype(bf16)
    got_wc1.wait()
    for index in range(4):
        columns = pl.ds(index * 256, 256)
        part = dot(v_slim[...], v_wc[:, columns], 1, 0)
        for a in range(4):
            for b in range(2):
                start = (2 * a + b) * share1
                v_p1[a, b, :, columns] = part[start : start + share1].astype(bf16)
    reduce_1.start()
    got_wc0 = load(wc_in.at[0], v_wc)
    unit_read2.turn()
    unit_read1.turn()
    reduce_1.turn()

    def conv_grad(part, taps, norm):
        for d in range(4):
            part[d] = dot(taps[...], norm[:, pl.ds(d * 256, 256)], 0, 0).astype(bf16)

    conv_grad(p_conv1, v_taps1, v_norm1)
    unit_conv1.start()
    reduce_1.finish()
    got_h1.wait()
    norm_backward(
        v_h1, lambda part: reduce_1.total(part), line[1:2], v_acc.at[1], v_gh, share1, share1
    )
    got_w2.wait()
    got_w1.wait()
    half = []
    for index in range(4):
        columns = pl.ds(index * 256, 256)
        value = (v_g[:, columns] + dot(v_gh[pl.ds(0, share1), :], v_w[1, :, columns], 1, 0)) * 0.25
        v_g[:, columns] = value
    low = v_g[...].astype(bf16)
    for index in range(4):
        columns = pl.ds(index * 256, 256)
        back = dot(low, v_w[0, :, columns], 1, 0)
        own = v_g[:, columns]
        grad_h = v_gh[pl.ds(0, share1), columns].astype(f32)
        for b in range(2):
            piece = slice(b * local, (b + 1) * local)
            v_a2s[2 * index + b, 0] = back[:, piece].astype(bf16)
            v_a2s[2 * index + b, 1] = own[:, piece].astype(bf16)
            v_a2s[2 * index + b, 2] = grad_h[:, piece].astype(bf16)
    swap_2 = swap_start(place, flight, v_a2s, v_a2r, as_.at[1], ar.at[1])
    got_w0 = load(w_in.at[0], v_w.at[1])
    unit_conv1.turn()
    reduce_ro.turn()

    def finish(which, stage, dst, step):
        which.copy.wait_recv()
        rows = which.last.shape[0]
        for start in range(0, rows, step):
            part = pl.ds(start, step)
            stage.out(which.total(part), dst.at[part])

    received(swap_2)

    gs0 = gathered(v_a2r, 0)
    gy0 = gathered(v_a2r, 1)
    gh1 = gathered(v_a2r, 2)
    got_conv0.wait()
    sums = []
    for image in range(images):
        rows = pl.ds(image * grid0, grid0)
        grad = dot(spread_mat[...], gs0[image * grid1 : (image + 1) * grid1], 1, 0)
        v_gs[rows, :] = grad
        conv = v_conv0[rows, :]
        sums.append(jnp.sum(grad * conv * jax.nn.sigmoid(conv), axis=0, keepdims=True))

    def fill_io():
        received_all([got_value] + got_mean)
        for d in range(4):
            columns = pl.ds(d * 256, 256)
            p_io[d, 128:256, :] = dot(gh1, v_value[:, columns], 0, 0).astype(bf16)
            p_io[d, 256:384, :] = (4.0 * dot(gy0, v_mean[:, columns], 0, 0)).astype(bf16)

    gate, grad_pooled = gate_back(0, sums, fill_io)
    masks = edge_masks(24)
    for image in range(images):
        rows = pl.ds(image * grid0, grid0)
        conv = v_conv0[rows, :]
        grad = v_gs[rows, :] * gate[image : image + 1]
        grad = grad + grad_pooled[image : image + 1] * (1.0 / grid0)
        grad = grad * silu_slope(conv, jax.nn.sigmoid(conv))
        taps_of(grad, v_zz0, v_taps0, image * grid0, 24, 24, masks)
    got_wc0.wait()
    for k in reduce_0.order:
        target = reduce_0.target(k)
        rows = pl.ds(pl.multiple_of(target * 2 * share0, 2 * share0), 2 * share0)
        for index in range(2):
            columns = pl.ds(index * 512, 512)
            part = dot(v_taps0[rows, :], v_wc[:, columns], 1, 0)
            for b in range(2):
                v_p0[target, b, :, columns] = part[b * share0 : (b + 1) * share0].astype(bf16)
        reduce_0.send_x(k)
    got_norm0.wait()
    conv_grad(p_conv0, v_taps0, v_norm0)
    unit_conv0.start()
    unit_io.start()
    unit_se.start()
    finish(unit_read2, stage_wide, o_read2, 64)
    finish(unit_read1, stage_half, o_read1, 256)
    unit_conv0.turn()
    unit_io.turn()
    unit_se.turn()
    reduce_0.turn()
    reduce_ro.finish()
    v_act[...] = (reduce_ro.total(pl.ds(0, v_act.shape[0])) + b_read2[...]).astype(bf16)
    out_ro = pltpu.make_async_copy(v_act, o_readout, store_sem.at[0])
    out_ro.start()
    finish(unit_conv1, stage_slim, o_conv.at[1], 384)
    reduce_0.finish()
    got_h0.wait()
    norm_backward(
        v_h0, lambda part: reduce_0.total(part), line[0:1], v_acc.at[0], v_gh, share0, 48
    )
    for index in range(8):
        v_a3s[index, 1] = v_gh[:, pl.ds(index * local, local)]
    swap_3 = swap_start(place, flight, v_a3s.at[:, 1], v_a3r.at[:, 1], as_.at[2], ar.at[2])
    for owner in range(8):
        columns = pl.ds(owner * local, local)
        for row, (which, kind) in enumerate(((0, 0), (1, 0), (0, 1), (1, 1))):
            v_lines_s[owner, row : row + 1, :] = jnp.sum(
                v_acc[which, kind, :, columns], axis=0, keepdims=True
            )
    got_w0.wait()
    for index in range(4):
        columns = pl.ds(index * 256, 256)
        grad = dot(v_gh[...], v_w[1, :, columns], 1, 0)
        for b in range(2):
            v_a3s[2 * index + b, 0] = grad[:, b * local : (b + 1) * local].astype(bf16)
    swap_4 = swap_start(place, flight, v_a3s.at[:, 0], v_a3r.at[:, 0], as_.at[3], ar.at[3])
    swap_5 = swap_start(place, flight, v_lines_s, v_lines_r, as_.at[4], ar.at[4])
    finish(unit_io, stage_slim, o_io.at[pl.ds(0, 384)], 384)
    finish(unit_se, stage_se, o_se, 4)
    received(swap_3)
    got_feats.wait()
    grad_h = v_a3r[:, 1].reshape(rows0, local)
    for d in range(4):
        p_in0[d] = dot(grad_h, v_feats[:, pl.ds(d * 256, 256)], 0, 0).astype(bf16)
    unit_in0.start()
    received(swap_5)
    total = v_lines_r[0]
    for s in range(1, 8):
        total = total + v_lines_r[s]
    for row in range(4):
        v_vec[4:5, row * 128 : row * 128 + 128] = total[row : row + 1]
    vec_copies = [
        flight.remote(v_vec, v_vec_r.at[k - 1], vs.at[k - 1], vr.at[k - 1], (lax.rem(dp + k, 4), mp))
        for k in (1, 2, 3)
    ]
    finish(unit_conv0, stage_slim, o_conv.at[0], 384)
    unit_in0.turn()
    received(swap_4)
    for image in range(images):
        rows = pl.ds(image * grid0, grid0)
        up = dot(spread_mat[...], gy0[image * grid1 : (image + 1) * grid1], 1, 0)
        v_gs[rows, :] = up + v_a3r[4 * image : 4 * image + 4, 0].reshape(grid0, local).astype(f32)
    out_feat = pltpu.make_async_copy(v_gs, o_features, store_sem.at[1])
    out_feat.start()
    received(vec_copies)
    o_vec[...] = v_vec[...] + v_vec_r[0] + v_vec_r[1] + v_vec_r[2]
    finish(unit_in0, stage_slim, o_io.at[pl.ds(384, 128)], 128)
    flight.drain()
    for stage in (stage_wide, stage_half, stage_slim, stage_se):
        stage.drain()
    out_ro.wait()
    out_feat.wait()


def received_all(copies):
    for copy in copies:
        copy.wait()


def run_backward(operands, smalls):
    def shaped(dtype, *dims):
        return jax.ShapeDtypeStruct(dims, dtype)

    outs = [
        shaped(bf16, 288, 512),
        shaped(f32, 1152, 128),
        shaped(f32, 512, 1024),
        shaped(f32, 256, 512),
        shaped(f32, 2, 1152, 256),
        shaped(f32, 512, 256),
        shaped(f32, 4, 64, 128),
        shaped(f32, 8, 512),
    ]

    def reducing(rows, columns):
        return [
            (bf16, 4, 2, rows, columns),
            (bf16, 4, rows, columns),
            (bf16, 3, rows, columns),
        ]

    def units(dtype, *dims):
        return [(dtype, 4) + dims, (dtype, 2) + dims, (dtype,) + dims]

    scratch = reducing(40, 1024) + reducing(288, 512) + reducing(40, 1024) + reducing(144, 1024)
    scratch += [
        (bf16, 288, 512),
        (bf16, 288, 512),
        (bf16, 288, 1024),
        (bf16, 4, 2, 288, 512),
        (bf16, 2, 1024, 1024),
        (bf16, 1152, 1024),
        (bf16, 1152, 1024),
        (bf16, 384, 1024),
        (f32, 1152, 128),
        (f32, 384, 128),
        (f32, 144, 1024),
        (f32, 40, 1024),
        (bf16, 320, 1024),
        (bf16, 320, 1024),
        (bf16, 320, 1024),
        (bf16, 1152, 1024),
        (f32, 40, 1024),
        (bf16, 8, 2, 40, 128),
        (bf16, 8, 2, 40, 128),
        (bf16, 8, 3, 40, 128),
        (bf16, 8, 3, 40, 128),
        (bf16, 8, 2, 144, 128),
        (bf16, 8, 2, 144, 128),
        (f32, 8, 4, 128),
        (f32, 8, 4, 128),
        (f32, 2, 8, 256),
        (f32, 2, 7, 8, 256),
        (f32, 1152, 128),
        (f32, 640, 128),
        (f32, 256, 128),
        (bf16, 1152, 1152),
        (bf16, 384, 1152),
        (bf16, 320, 1152),
        (f32, 2, 2, 8, 1024),
        (bf16, 144, 1024),
        (f32, 8, 512),
        (f32, 3, 8, 512),
    ]
    scratch += units(bf16, 512, 1024) + units(bf16, 256, 512)
    scratch += units(bf16, 1152, 256) + units(bf16, 1152, 256)
    scratch += units(bf16, 384, 256) + units(bf16, 128, 256) + units(f32, 4, 64, 128)
    scratch += [
        (f32, 2, 64, 1024),
        (f32, 1, 256, 512),
        (f32, 2, 384, 256),
        (f32, 1, 4, 64, 128),
    ]
    dma = pltpu.SemaphoreType.DMA
    sems = [(48,), (2,), (4, 2), (4, 4), (4, 4), (4, 4), (4, 4), (5, 7), (5, 7), (2, 7), (2, 7)]
    sems += [(7, 2), (7, 2), (7,), (7,), (3,), (3,)]
    anywhere = [pl.BlockSpec(memory_space=pl.ANY)]
    return pl.pallas_call(
        backward_kernel,
        name="backward",
        out_shape=outs,
        in_specs=anywhere * len(operands) + vmem_specs(len(smalls)),
        out_specs=anywhere * (len(outs) - 1) + vmem_specs(1),
        scratch_shapes=[pltpu.VMEM(dims, dtype) for dtype, *dims in scratch]
        + [dma(shape) for shape in sems],
        compiler_params=pltpu.CompilerParams(
            collective_id=21, has_side_effects=True, vmem_limit_bytes=63 << 20
        ),
    )(*operands, *smalls)


def on_device(
    mp_size,
    dp_size,
    features,
    w_in,
    ln_gain,
    ln_bias,
    w_conv,
    se_down,
    se_down_bias,
    se_up,
    se_up_bias,
    w_out,
    w_read1,
    b_read1,
    w_read2,
    b_read2,
    out_grad,
    box_counts,
):
    images, side, _, width = features.shape
    half = side // 2
    local = w_in.shape[1]
    rows = (images * side * side, images * half * half)
    sides = (side, half)
    share = (rows[0] // mp_size, rows[1] // mp_size)
    mp = lax.axis_index("mp")

    def ex(name, collective, *pairs):
        return exchange(name, collective, mp_size, *pairs)

    feats = features.reshape(rows[0], width)
    grad_top = (
        out_grad.astype(f32) * box_counts.astype(f32)[:, None, None, None]
    ).astype(bf16).reshape(rows[1], -1)
    grad_b_read2 = jnp.sum(grad_top.astype(f32), axis=0)
    weights, vectors = gather_weights(
        mp_size,
        jnp.stack([w_in[0], w_out[0], w_in[1], w_out[1]]),
        jnp.concatenate([ln_gain, ln_bias], axis=0),
    )
    (grad_full,) = ex("gather_dout", 3, ("ag", grad_top))
    wide_in = (weights[0], weights[2])
    wide_out = (weights[1], weights[3])
    vectors = jnp.swapaxes(vectors, 0, 1).reshape(4, width)
    gains, shifts = vectors[:2], vectors[2:]

    def forward(index, low):
        h = nt(low, wide_in[index])
        normed, inv_std = normalize(h)
        norm = (normed * gains[index] + shifts[index]).astype(bf16)
        conv = conv_forward(norm, w_conv[index], images, sides[index])
        act = jax.nn.silu(conv)
        pooled = jnp.mean(act, axis=1)
        (pre_down,) = ex(
            "squeeze", 4 + index, ("psum", exact(pooled, se_down[index].astype(f32)))
        )
        pre_down = pre_down + se_down_bias[index]
        squeeze = jax.nn.silu(pre_down)
        excite = jax.nn.sigmoid(exact(squeeze, se_up[index].astype(f32)) + se_up_bias[index])
        scaled = act * excite[:, None, :]
        own_h = row_share(h, mp * share[index], share[index])
        return norm, conv, act, pooled, pre_down, squeeze, excite, scaled, own_h

    first = forward(0, feats)
    mean_scaled = pool(first[7].reshape(rows[0], -1), images, side).astype(bf16)
    (mean_scaled,) = ex("gather_scaled0", 6, ("ag", mean_scaled))
    mean_scaled = blocks_to_wide(mean_scaled)
    value = pool(feats, images, side) + nt(mean_scaled, wide_out[0])
    value_low = value.astype(bf16)
    second = forward(1, value_low)
    (scaled1,) = ex("gather_scaled1", 7, ("ag", second[7].reshape(rows[1], -1).astype(bf16)))
    scaled1 = blocks_to_wide(scaled1)
    top = (value + nt(scaled1, wide_out[1])).astype(bf16)
    act_full, slope = gelu_parts(nn(top, w_read1) + b_read1)
    act_low = act_full.astype(bf16)
    grad_full = blocks_to_wide(grad_full)
    grad_pre = (nt(grad_full, w_read2) * slope).astype(bf16)
    grad_b_read1 = jnp.sum(grad_pre.astype(f32), axis=0)
    (grad_out,) = ex(
        "scatter_g", 8, ("rs", nt(grad_pre, w_read1).astype(bf16).reshape(mp_size, share[1], width))
    )
    (readout,) = ex(
        "scatter_readout", 9, ("rs", wide_to_blocks(nn(act_low, w_read2).astype(bf16), mp_size))
    )
    readout = (readout + b_read2).astype(bf16).reshape(images, half, half, -1)
    grad_w_read2 = tn(act_low, grad_full)
    grad_w_read1 = tn(top, grad_pre)

    def to_channels(name, collective, *values):
        stacked = jnp.concatenate([wide_to_blocks(value, mp_size) for value in values], axis=1)
        (result,) = ex(name, collective, ("a2a", stacked))
        parts, start = [], 0
        for value in values:
            part = result[:, start : start + value.shape[0]]
            start += value.shape[0]
            parts.append(part)
        return parts

    def backward(index, grad_scaled, saved):
        norm, conv, act, pooled, pre_down, squeeze, excite, scaled, own_h = saved
        here = sides[index]
        gate_grad = jnp.sum(grad_scaled * act, axis=1)
        grad_up = gate_grad * excite * (1.0 - excite)
        (grad_squeeze,) = ex(
            "squeeze_back", 10 + index, ("psum", exact(grad_up, se_up[index].astype(f32).T))
        )
        grad_down = grad_squeeze * silu_grad(pre_down)
        grad_pooled = exact(grad_down, se_down[index].astype(f32).T)
        grad_act = grad_scaled * excite[:, None, :] + grad_pooled[:, None, :] / (here * here)
        grad_conv = (grad_act * silu_grad(conv)).astype(bf16).reshape(rows[index], -1)
        taps = shifted(grad_conv, images, here)
        grad_w_conv = tn(taps, norm).reshape(9, local, width)
        taps_weight = jnp.swapaxes(w_conv[index], 0, 1).reshape(9 * local, width)
        partial_norm = nn(taps, taps_weight).astype(bf16)
        (grad_norm,) = ex(
            "scatter_norm", 12 + index, ("rs", partial_norm.reshape(mp_size, share[index], width))
        )
        normed, inv_std = normalize(own_h)
        grad_gain = jnp.sum(grad_norm * normed, axis=0)
        grad_shift = jnp.sum(grad_norm, axis=0)
        scaled_grad = grad_norm * gains[index]
        grad_h = (
            inv_std
            * (
                scaled_grad
                - jnp.mean(scaled_grad, axis=1, keepdims=True)
                - normed * jnp.mean(scaled_grad * normed, axis=1, keepdims=True)
            )
        ).astype(bf16)
        small = (
            exact(squeeze.T, grad_up),
            jnp.sum(grad_up, axis=0),
            exact(pooled.T, grad_down),
            jnp.sum(grad_down, axis=0),
        )
        return grad_w_conv, grad_h, jnp.stack([grad_gain, grad_shift]), small

    grad_low = grad_out.astype(bf16)
    gs1, gy1 = to_channels("spread1", 14, nn(grad_low, wide_out[1]).astype(bf16), grad_low)
    gs1 = gs1.astype(f32).reshape(images, half * half, local)
    grad_w_out1 = tn(gy1.reshape(rows[1], local), scaled1)
    grad_w_conv1, grad_h1, lines1, small1 = backward(1, gs1, second)
    grad_value = (grad_out + nn(grad_h1, wide_in[1])) * 0.25
    grad_value_low = grad_value.astype(bf16)
    gs0, gy0, gh1 = to_channels(
        "spread0", 15, nn(grad_value_low, wide_out[0]).astype(bf16), grad_value_low, grad_h1
    )
    grad_w_in1 = tn(gh1.reshape(rows[1], local), value_low)
    grad_w_out0 = 4.0 * tn(gy0.reshape(rows[1], local), mean_scaled)
    residual = spread(gy0.astype(f32).reshape(rows[1], local), images, half)
    gs0 = spread(gs0.astype(f32).reshape(rows[1], local), images, half)
    grad_w_conv0, grad_h0, lines0, small0 = backward(
        0, gs0.reshape(images, side * side, local), first
    )
    grad_in = nn(grad_h0, wide_in[0]).astype(bf16)
    lines = jnp.concatenate([lines0, lines1], axis=0)
    stacked = jnp.concatenate(
        [wide_to_blocks(grad_in, mp_size), wide_to_blocks(grad_h0, mp_size)], axis=1
    )
    spread_all, lines = ex(
        "spread_last", 16, ("a2a", stacked), ("rs", wide_to_blocks(lines, mp_size))
    )
    grad_features = spread_all[:, : share[0]].astype(f32).reshape(rows[0], local) + residual
    grad_features = grad_features.reshape(images, side, side, local)
    grad_w_in0 = tn(spread_all[:, share[0] :].reshape(rows[0], local), feats)

    def parted(value, axis):
        shape = value.shape
        split = value.reshape(shape[:axis] + (dp_size, shape[axis] // dp_size) + shape[axis + 1 :])
        return jnp.moveaxis(split, axis, 0)

    scattered = dp_scatter(
        dp_size,
        [
            parted(jnp.stack([grad_w_in0, grad_w_in1]).astype(bf16), 2),
            parted(jnp.stack([grad_w_conv0, grad_w_conv1]).astype(bf16), 3),
            parted(jnp.stack([small0[2], small1[2]]).astype(bf16), 2),
            parted(jnp.stack([small0[0], small1[0]]).astype(bf16), 1),
            parted(jnp.stack([grad_w_out0, grad_w_out1]).astype(bf16), 2),
            parted(grad_w_read1.astype(bf16), 0),
            parted(grad_w_read2.astype(bf16), 1),
        ],
    )
    vectors = lax.psum(
        (
            lines[0::2],
            lines[1::2],
            jnp.stack([small0[3], small1[3]]),
            jnp.stack([small0[1], small1[1]]),
            grad_b_read1,
            grad_b_read2,
        ),
        "dp",
    )
    return (
        readout,
        grad_features,
        scattered[0],
        vectors[0],
        vectors[1],
        jnp.swapaxes(scattered[1], 1, 2),
        scattered[2],
        vectors[2],
        scattered[3],
        vectors[3],
        scattered[4],
        scattered[5],
        vectors[4],
        scattered[6],
        vectors[5],
    )


def on_device_fast(
    features,
    w_in,
    ln_gain,
    ln_bias,
    w_conv,
    se_down,
    se_down_bias,
    se_up,
    se_up_bias,
    w_out,
    w_read1,
    b_read1,
    w_read2,
    b_read2,
    out_grad,
    box_counts,
):
    feats = features.reshape(1152, 1024)
    grad_top = (
        out_grad.astype(f32) * box_counts.astype(f32)[:, None, None, None]
    ).astype(bf16).reshape(288, 512)
    wc = jnp.swapaxes(w_conv, 1, 2).reshape(2, 1152, 1024)
    mats = selections()
    (
        norm0,
        norm1,
        conv0,
        conv1,
        gates,
        own_h0,
        own_h1,
        mean_scaled,
        scaled1,
        value_low,
        top,
        act_low,
        grad_pre,
        grad_out,
        weights,
        lines,
        grad_full,
        partial_out,
    ) = run_forward(
        feats,
        w_in,
        w_out,
        wc,
        grad_top,
        w_read1,
        w_read2,
        jnp.concatenate([ln_gain, ln_bias], axis=0),
        (se_down, se_down_bias, se_up, se_up_bias, b_read1.reshape(1, -1)),
        mats,
    )
    readout, grad_features, read2, read1, conv, others, gates_grad, vectors = run_backward(
        (
            grad_out.reshape(4, 2, 40, 1024),
            partial_out.reshape(4, 2, 288, 512),
            act_low,
            grad_pre,
            top,
            grad_full,
            weights.reshape(4, 1024, 1024),
            norm0,
            norm1,
            conv0,
            conv1,
            own_h0,
            own_h1,
            mean_scaled,
            scaled1,
            value_low,
            feats,
            wc,
        ),
        (
            gates,
            lines,
            se_down,
            se_up,
            b_read2.reshape(1, -1),
            mats[1],
            mats[2],
            4.0 * mats[0].T,
        ),
    )
    others = others.reshape(4, 128, 256)
    gates_grad = gates_grad.reshape(2, 2, 64, 128)
    return (
        readout.reshape(2, 12, 12, 512),
        grad_features.reshape(2, 24, 24, 128),
        jnp.stack([others[3], others[1]]),
        vectors[4, :256].reshape(2, 128),
        vectors[4, 256:].reshape(2, 128),
        jnp.swapaxes(conv.reshape(2, 9, 128, 256), 1, 2),
        jnp.swapaxes(gates_grad[:, 0], 1, 2),
        vectors[2].reshape(2, 256),
        gates_grad[:, 1],
        vectors[3, :256].reshape(2, 128),
        jnp.stack([others[2], others[0]]),
        read1,
        vectors[0],
        read2,
        vectors[1],
    )


def solution(mesh):
    in_specs = (
        P("dp", None, None, None),
        P(None, "mp", None),
        P(None, "mp"),
        P(None, "mp"),
        P(None, "mp", None, None),
        P(None, "mp", None),
        P(),
        P(None, None, "mp"),
        P(None, "mp"),
        P(None, "mp", None),
        P(None, "mp"),
        P("mp"),
        P("mp", None),
        P("mp"),
        P("dp", None, None, "mp"),
        P("dp"),
    )
    out_specs = (
        P("dp", None, None, "mp"),
        P("dp", None, None, "mp"),
        P(None, "mp", "dp"),
        P(None, "mp"),
        P(None, "mp"),
        P(None, "mp", None, "dp"),
        P(None, "mp", "dp"),
        P(),
        P(None, "dp", "mp"),
        P(None, "mp"),
        P(None, "mp", "dp"),
        P("dp", "mp"),
        P("mp"),
        P("mp", "dp"),
        P("mp"),
    )
    if mesh.shape["mp"] == 8 and mesh.shape["dp"] == 4:
        body = on_device_fast
    else:
        body = partial(on_device, mesh.shape["mp"], mesh.shape["dp"])
    return jax.shard_map(
        body, mesh=mesh, in_specs=in_specs, out_specs=out_specs, check_vma=False
    )
```
